32 devices in a mesh: row: 8 (over y, x, core), col: 4 (over z).
Axes of the slice: x: 2, y: 2, z: 4, core: 2. Of those that a mesh axis runs over, the one named last changes fastest.
Arguments:
- tokens: bfloat16 [8192, 2048], P('row', 'col'), may hold values from -6 to 6
- norm_attn: bfloat16 [2048], P('col'), may hold values from 0.099609375 to 1.8984375
- norm_query: bfloat16 [2048], P('col'), may hold values from 0.099609375 to 1.8984375
- norm_key: bfloat16 [2048], P('col'), may hold values from 0.099609375 to 1.8984375
- norm_moe: bfloat16 [2048], P('col'), may hold values from 0.099609375 to 1.8984375
- w_query: bfloat16 [2048, 2048], P('row', 'col'), may hold values from -0.125 to 0.125
- w_key: bfloat16 [2048, 2048], P('row', 'col'), may hold values from -0.125 to 0.125
- w_value: bfloat16 [2048, 2048], P('row', 'col'), may hold values from -0.125 to 0.125
- w_out: bfloat16 [2048, 2048], P('row', 'col'), may hold values from -1.5 to 1.5
- w_router: bfloat16 [2048, 16], P('row', 'col'), may hold values from -0.0625 to 0.0625
- w_gate: bfloat16 [2048, 16, 1024], P('row', None, 'col'), may hold values from -0.125 to 0.125
- w_up: bfloat16 [2048, 16, 1024], P('row', None, 'col'), may hold values from -0.125 to 0.125
- w_down: bfloat16 [2048, 16, 1024], P('row', None, 'col'), may hold values from -0.5 to 0.5
- routes: int32 [8192, 8], P('row'), may hold values from 0 to 15, all different within a row; in each aligned block of 1024 rows (0 to 1023, 1024 to 2047, ...) at most 640 rows name the same one
- span_starts: int32 [8, 2], P('row'), may hold values from 0 to 768, as said below
- cotangent: bfloat16 [8192, 2048], P('row', 'col'), may hold values from -6 to 6
Outputs:
- output: bfloat16 [8192, 2048], P('row', 'col')
- d_tokens: float32 [8192, 2048], P('row', 'col')
- d_norm_attn: float32 [2048], P('col')
- d_norm_query: float32 [2048], P('col')
- d_norm_key: float32 [2048], P('col')
- d_norm_moe: float32 [2048], P('col')
- d_w_query: float32 [2048, 2048], P('row', 'col')
- d_w_key: float32 [2048, 2048], P('row', 'col')
- d_w_value: float32 [2048, 2048], P('row', 'col')
- d_w_out: float32 [2048, 2048], P('row', 'col')
- d_w_router: float32 [2048, 16], P('row', 'col')
- d_w_gate: float32 [2048, 16, 1024], P('row', None, 'col')
- d_w_up: float32 [2048, 16, 1024], P('row', None, 'col')
- d_w_down: float32 [2048, 16, 1024], P('row', None, 'col')
The draws below stay inside these ranges and needn't reach their ends.
Inputs may be any that keep to these rules, and one draw needn't show every extreme that they name: `routes`: each row names 8 different experts; among the 1024 rows of one sequence no expert is named more than 640 times. `span_starts`: span k of a sequence (k from 0) starts between k * 2 * 256 and k * 2 * 256 + 256; the spans of a sequence are disjoint and lie within it.
All inputs are finite; a program needn't handle non-finite values.
Results may differ from the reference program's by a relative error of at most 0.014.
The reference program's roundings to bfloat16 on the way count: a program that leaves them out, or rounds other values in their place, can miss the bound.
Values may be sent and summed in bfloat16 or wider, within the bound.
A program may use at most 384 MiB of HBM per device.

```python
import math
import jax
import jax.numpy as jnp
import numpy as np
from jax import lax

D = 2048
FF = 1024
HEADS = 16
HD = 128
TOP = 8
EXPERTS = 16
IMG = 256
SEQ_LEN = 1024
SPANS = 2
CAP = 640
SEQS = 8
TOKENS = 8192


def draw_span_starts(key, part):
    region = SEQ_LEN // SPANS
    offsets = jax.random.randint(key, (SEQS, SPANS), 0, region - IMG + 1, dtype=jnp.int32)
    bases = jnp.arange(SPANS, dtype=jnp.int32) * region
    return (bases[None, :] + offsets).astype(jnp.int32)


def shard_levels(own_key, shape, pieces, smallest, largest):
    level = 1.0
    for axis_at, shards_of in pieces:
        steps = jax.random.uniform(jax.random.fold_in(jax.random.fold_in(own_key, 6), axis_at), (shards_of,), jnp.float32, smallest / len(pieces), largest / len(pieces))
        level = level * jnp.repeat(jnp.exp(steps), shape[axis_at] // shards_of).reshape((-1,) + (1,) * (len(shape) - 1 - axis_at))
    return level


def assign_block(own_key, own, number, rows, number_of, top, limit, lean):
    ranking = jax.random.permutation(own_key, number_of)
    crowded, ordinary = shares(number_of, rows * top, limit, lean, True), shares(number_of, rows * top, limit, lean, False)
    places = jnp.arange(number_of)

    def named(tallies, rotation):
        used = int((tallies > 0).sum())
        fixed = max(1, used // 4)
        passed = fixed + (places - fixed + rotation * (used - fixed)) % max(1, number_of - fixed)
        return jnp.zeros((number_of,), jnp.int32).at[ranking[jnp.where(places < fixed, places, passed)]].set(jnp.asarray(tallies, jnp.int32))

    tallies = jnp.where(number % 4 == 0, named(crowded, number // 4), named(ordinary, number - number // 4 - 1))
    mixed = jax.random.permutation(jax.random.fold_in(own, 3), number_of)
    source_of, sink = mixed[0:number_of // 2 * 2:2], mixed[1:number_of // 2 * 2:2]
    margin = jnp.minimum(tallies[source_of] - 1, limit - tallies[sink]) // 2
    margin = jnp.where((source_of == ranking[0]) | (sink == ranking[0]) | (tallies[sink] == 0), 0, jnp.maximum(margin, 0))
    passed = jax.random.randint(jax.random.fold_in(own, 4), (number_of // 2,), 0, 1 << 20) % (margin + 1)
    tallies = tallies.at[source_of].add(-passed).at[sink].add(passed)
    labels = jnp.searchsorted(jnp.cumsum(tallies), jnp.arange(rows * top), side="right").astype(jnp.int32)
    table = labels.reshape(top, rows).T
    table = table[jax.random.permutation(jax.random.fold_in(own, 1), rows)]
    rotation = jax.random.randint(jax.random.fold_in(own, 2), (rows, 1), 0, top)
    return jnp.take_along_axis(table, (jnp.arange(top)[None, :] + rotation) % top, axis=1)


def shares(count, total, most, lean, full):
    loads = [(1 << 20) // math.isqrt(grade ** lean) + 1 for grade in range(1, count + 1)]
    largest = most if full else min(most, max(-(-total // count), total * loads[0] // sum(loads)))
    least = 1 if total - largest >= count - 1 else 0
    given, surplus = [largest] + [least] * (count - 1), total - largest - least * (count - 1)
    while surplus > 0:
        free = [i for i in range(1, count) if given[i] < largest] or [i for i in range(1, count) if given[i] < most]
        pool, left = sum([loads[i] for i in free]), surplus
        for i in free:
            extra = min(most - given[i], max(1, left * loads[i] // pool), surplus)
            given[i] = given[i] + extra
            surplus = surplus - extra
    return np.array(given)


def normal_values(key, shape, width, bound, pieces=(), kind=jnp.bfloat16):
    level = shard_levels(key, shape, pieces, -0.22, 0.18) if pieces else 1.0
    values = jax.random.normal(key, shape, jnp.float32) * width * level
    return jnp.minimum(jnp.maximum(values, -bound), bound).astype(kind)


def setup_inputs(seed: int = 0) -> dict:
    seeds = jax.random.split(jax.random.key(seed), 17)
    tokens = normal_values(seeds[0], (TOKENS, D), 1.0, 6.0, ((0, 8), (1, 4)))
    norm_attn = jnp.clip(1.0 + 0.18 * jax.random.normal(seeds[1], (D,), jnp.float32), 0.099609375, 1.8984375).astype(jnp.bfloat16)
    norm_query = jnp.clip(1.0 + 0.18 * jax.random.normal(seeds[2], (D,), jnp.float32), 0.099609375, 1.8984375).astype(jnp.bfloat16)
    norm_key = jnp.clip(1.0 + 0.18 * jax.random.normal(seeds[3], (D,), jnp.float32), 0.099609375, 1.8984375).astype(jnp.bfloat16)
    norm_moe = jnp.clip(1.0 + 0.18 * jax.random.normal(seeds[4], (D,), jnp.float32), 0.099609375, 1.8984375).astype(jnp.bfloat16)
    w_query = normal_values(seeds[5], (D, D), D ** -0.5, 0.125, ((0, 8), (1, 4)))
    w_key = normal_values(seeds[6], (D, D), D ** -0.5, 0.125, ((0, 8), (1, 4)))
    w_value = normal_values(seeds[7], (D, D), D ** -0.5, 0.125, ((0, 8), (1, 4)))
    w_out = normal_values(seeds[8], (D, D), (D // 128) ** -0.5, 1.5, ((0, 8), (1, 4)))
    w_router = normal_values(seeds[9], (D, EXPERTS), (4 * D) ** -0.5, 0.0625, ((0, 8), (1, 4)))
    w_gate = normal_values(seeds[10], (D, EXPERTS, FF), D ** -0.5, 0.125, ((0, 8), (2, 4)))
    w_up = normal_values(seeds[11], (D, EXPERTS, FF), D ** -0.5, 0.125, ((0, 8), (2, 4)))
    w_down = normal_values(seeds[12], (D, EXPERTS, FF), (FF // 9) ** -0.5, 0.5, ((0, 8), (2, 4)))
    routes_keys = jax.random.split(jax.random.fold_in(seeds[13], 1), TOKENS // SEQ_LEN)
    routes_turns = jax.random.permutation(jax.random.fold_in(seeds[13], 3), TOKENS // SEQ_LEN)
    routes = jax.vmap(lambda own, number: assign_block(jax.random.fold_in(seeds[13], 2), own, number, SEQ_LEN, EXPERTS, TOP, CAP, 1))(routes_keys, routes_turns).reshape((TOKENS, TOP))
    span_starts = draw_span_starts(jax.random.fold_in(seeds[16], 71), 0)
    cotangent = normal_values(seeds[15], (TOKENS, D), 1.0, 6.0, ((0, 8), (1, 4)))
    return dict(tokens=tokens, norm_attn=norm_attn, norm_query=norm_query, norm_key=norm_key, norm_moe=norm_moe, w_query=w_query, w_key=w_key, w_value=w_value, w_out=w_out, w_router=w_router, w_gate=w_gate, w_up=w_up, w_down=w_down, routes=routes, span_starts=span_starts, cotangent=cotangent)


EPSILON = 1e-05
ROPE_BASE = 10000.0
MASKED = -1e+30
PRECISE = lax.Precision.HIGHEST

@jax.custom_vjp
def low(v):
    return lax.optimization_barrier(v.astype(jnp.bfloat16)).astype(jnp.float32)

@jax.custom_vjp
def low_back(v):
    return v

def low_keep(v):
    return (low(v), None)

def low_pass(kept, grad):
    return (grad,)

def back_keep(v):
    return (v, None)

def back_low(kept, grad):
    return (low(grad),)
low.defvjp(low_keep, low_pass)
low_back.defvjp(back_keep, back_low)

def matmul(left, right):
    return jnp.dot(left, right, precision=PRECISE, preferred_element_type=jnp.float32)

def normalize(values, gain):
    return values * lax.rsqrt(lax.optimization_barrier(jnp.mean(values * values, axis=-1, keepdims=True)) + EPSILON) * gain

def rope_tables(length):
    half_size = HD // 2
    places = jnp.arange(length, dtype=jnp.float32)
    rates = jnp.exp(-math.log(ROPE_BASE) * jnp.arange(half_size, dtype=jnp.float32) / half_size)
    angles = places[:, None] * rates[None, :]
    return (jnp.cos(angles), jnp.sin(angles))

def rotate(values, cosine, sine):
    half_size = HD // 2
    first_half = values[..., :half_size]
    second_half = values[..., half_size:]
    cos_part = cosine[:, None, :]
    sin_part = sine[:, None, :]
    return jnp.concatenate([first_half * cos_part - second_half * sin_part, second_half * cos_part + first_half * sin_part], axis=-1)

def span_ids(starts):
    places = jnp.arange(SEQ_LEN, dtype=jnp.int32)
    inside = (places[None, :] >= starts[:, None]) & (places[None, :] < starts[:, None] + IMG)
    numbers = jnp.arange(1, starts.shape[0] + 1, dtype=jnp.int32)
    return lax.optimization_barrier(jnp.sum(jnp.where(inside, numbers[:, None], 0), axis=0)).astype(jnp.int32)

def attend(packed):
    query_seq, key_seq, value_seq, starts = packed
    scale = 1.0 / math.sqrt(HD)
    scores = low_back(jnp.einsum('qhd,khd->hqk', query_seq, key_seq, precision=PRECISE) * scale)
    span_of = span_ids(starts)
    places = jnp.arange(SEQ_LEN, dtype=jnp.int32)
    allowed = (places[None, :] <= places[:, None]) | (span_of[:, None] == span_of[None, :]) & (span_of[:, None] > 0)
    scores = jnp.where(allowed[None], scores, MASKED)
    probs = low(jax.nn.softmax(scores, axis=-1))
    mixed = jnp.einsum('hqk,khd->qhd', probs, value_seq, precision=PRECISE)
    return mixed.reshape(SEQ_LEN, D)

def forward(tokens, norm_attn, norm_query, norm_key, norm_moe, w_query, w_key, w_value, w_out, w_router, w_gate, w_up, w_down, routes, span_starts):
    normed_attn = low(normalize(tokens, norm_attn))
    query_raw = low_back(matmul(normed_attn, w_query))
    key_raw = low_back(matmul(normed_attn, w_key))
    value_low = low(low_back(matmul(normed_attn, w_value)))
    cosine, sine = rope_tables(SEQ_LEN)
    queries = low(rotate(normalize(query_raw, norm_query).reshape(SEQS, SEQ_LEN, HEADS, HD), cosine, sine))
    keys = low(rotate(normalize(key_raw, norm_key).reshape(SEQS, SEQ_LEN, HEADS, HD), cosine, sine))
    value_heads = value_low.reshape(SEQS, SEQ_LEN, HEADS, HD)
    mixed = lax.map(jax.checkpoint(attend), (queries, keys, value_heads, span_starts))
    mixed = low(low_back(mixed.reshape(SEQS * SEQ_LEN, D)))
    attn = low_back(matmul(mixed, w_out.T))
    hidden_state = tokens + attn
    normed_moe = low(normalize(hidden_state, norm_moe))
    logits = low_back(matmul(normed_moe, w_router))
    router_probs = jax.nn.softmax(logits, axis=-1)
    routed = jnp.any(routes[:, :, None] == jnp.arange(EXPERTS, dtype=jnp.int32)[None, None, :], axis=1)
    gate_table = jnp.where(routed, router_probs, 0.0)

    def expert_step(total, packed):
        gate_mat, up_mat, down_mat, column = packed
        gate_pre = low_back(matmul(normed_moe, gate_mat))
        up_pre = low_back(matmul(normed_moe, up_mat))
        hidden = low(column[:, None] * jax.nn.silu(gate_pre) * up_pre)
        return (total + matmul(hidden, down_mat.T), None)
    packed = (jnp.moveaxis(w_gate, 1, 0), jnp.moveaxis(w_up, 1, 0), jnp.moveaxis(w_down, 1, 0), gate_table.T)
    moe, unused = lax.scan(jax.checkpoint(expert_step), jnp.zeros_like(tokens), packed)
    return hidden_state + low_back(moe)

def reference(tokens, norm_attn, norm_query, norm_key, norm_moe, w_query, w_key, w_value, w_out, w_router, w_gate, w_up, w_down, routes, span_starts, cotangent):
    floats = (tokens.astype(jnp.float32), norm_attn.astype(jnp.float32), norm_query.astype(jnp.float32), norm_key.astype(jnp.float32), norm_moe.astype(jnp.float32), w_query.astype(jnp.float32), w_key.astype(jnp.float32), w_value.astype(jnp.float32), w_out.astype(jnp.float32), w_router.astype(jnp.float32), w_gate.astype(jnp.float32), w_up.astype(jnp.float32), w_down.astype(jnp.float32))

    def fixed(*values):
        return forward(*values, routes, span_starts)
    result, pullback = jax.vjp(fixed, *floats)
    grads = pullback(cotangent.astype(jnp.float32))
    d_tokens, d_norm_attn, d_norm_query, d_norm_key, d_norm_moe, d_w_query, d_w_key, d_w_value, d_w_out, d_w_router, d_w_gate, d_w_up, d_w_down = grads
    return (result.astype(jnp.bfloat16), d_tokens, d_norm_attn, d_norm_query, d_norm_key, d_norm_moe, d_w_query, d_w_key, d_w_value, d_w_out, d_w_router, d_w_gate, d_w_up, d_w_down)
```

```python
import functools
import math

import jax
import jax.numpy as jnp
from jax import lax
from jax.experimental import pallas as pl
from jax.experimental.layout import Layout, with_layout_constraint
from jax.experimental.pallas import tpu as pltpu
from jax.sharding import PartitionSpec as P

HD = 128
IMG = 256

EPSILON = 1e-05
ROPE_BASE = 10000.0
MASKED = -1e30
VMEM_LIMIT = 66_000_000
BF = jnp.bfloat16
F32 = jnp.float32


def dot_nn(a, b):
    return lax.dot_general(a, b, (((1,), (0,)), ((), ())), preferred_element_type=F32)


def dot_nt(a, b):
    return lax.dot_general(a, b, (((1,), (1,)), ((), ())), preferred_element_type=F32)


def dot_tn(a, b):
    return lax.dot_general(a, b, (((0,), (0,)), ((), ())), preferred_element_type=F32)


def row_major(values):
    return with_layout_constraint(values, Layout(major_to_minor=tuple(range(values.ndim))))


def after(values, *others):
    return lax.optimization_barrier((values, *others))[0]


def line_pairs():
    n = lax.axis_size("col")
    return n, [(i, i + 1) for i in range(n - 1)], [(i + 1, i) for i in range(n - 1)]


def gather_line(block):
    n, to_right, to_left = line_pairs()
    me = lax.axis_index("col")
    from_left, from_right = [block], [block]
    for _ in range(n - 1):
        from_left.append(lax.ppermute(from_left[-1], "col", to_right))
        from_right.append(lax.ppermute(from_right[-1], "col", to_left))
    out = jnp.zeros((n, *block.shape), block.dtype)
    out = lax.dynamic_update_index_in_dim(out, block, me, 0)
    for r in range(1, n):
        piece = from_left[r] + from_right[n - r]
        out = lax.dynamic_update_index_in_dim(out, piece, lax.rem(me - r + n, n), 0)
    return out


def scatter_line(part):
    n, to_right, to_left = line_pairs()
    me = lax.axis_index("col")
    right = left = None
    for r in range(1, n):
        k = n - r
        go_right = part(jnp.minimum(me + k, n - 1))
        go_left = part(jnp.maximum(me - k, 0))
        if right is not None:
            go_right = go_right + right.astype(F32)
            go_left = go_left + left.astype(F32)
        right = lax.ppermute(go_right.astype(BF), "col", to_right)
        left = lax.ppermute(go_left.astype(BF), "col", to_left)
    return part(me) + right.astype(F32) + left.astype(F32)


def sum_small(values):
    n = lax.axis_size("col")
    total = values
    for k in range(1, n):
        total = total + lax.ppermute(values, "col", [(i, (i + k) % n) for i in range(n)])
    return total


def gather_small(values):
    n = lax.axis_size("col")
    me = lax.axis_index("col")
    out = jnp.zeros((n, *values.shape), values.dtype)
    out = lax.dynamic_update_index_in_dim(out, values, me, 0)
    for k in range(1, n):
        piece = lax.ppermute(values, "col", [(i, (i + k) % n) for i in range(n)])
        out = lax.dynamic_update_index_in_dim(out, piece, lax.rem(me - k + n, n), 0)
    return out


def rope_tables(length):
    half_size = HD // 2
    places = jnp.arange(length, dtype=F32)
    rates = jnp.exp(-math.log(ROPE_BASE) * jnp.arange(half_size, dtype=F32) / half_size)
    angles = places[:, None] * rates[None, :]
    cosine, sine = jnp.cos(angles), jnp.sin(angles)
    return jnp.concatenate([cosine, cosine], 1), jnp.concatenate([-sine, sine], 1)


def span_ids(starts, length):
    places = jnp.arange(length, dtype=jnp.int32)
    inside = (places[None, :] >= starts[:, None]) & (places[None, :] < starts[:, None] + IMG)
    numbers = jnp.arange(1, starts.shape[0] + 1, dtype=jnp.int32)
    return jnp.sum(jnp.where(inside, numbers[:, None], 0), axis=0)


def attend_kernel(
    scale, block, q_ref, k_ref, v_ref, iq_ref, ik_ref, gq_ref, gk_ref, cos_ref, sin_ref,
    srow_ref, scol_ref, qo_ref, ko_ref, vo_ref, mixed_ref
):
    rows = q_ref.shape[0]
    cosine, sine = cos_ref[...], sin_ref[...]

    def turned(raw_ref, inv_ref, gain_ref):
        normed = raw_ref[...] * inv_ref[...] * gain_ref[...].astype(F32)
        return (normed * cosine + pltpu.roll(normed, HD // 2, 1) * sine).astype(BF)

    qo_ref[...] = turned(q_ref, iq_ref, gq_ref)
    ko_ref[...] = turned(k_ref, ik_ref, gk_ref)
    vo_ref[...] = v_ref[...].astype(BF)
    for first in range(0, rows, block):
        last = min(rows, first + block + IMG)
        scores = dot_nt(qo_ref[first : first + block, :], ko_ref[:last, :]) * scale
        q_at = first + lax.broadcasted_iota(jnp.int32, scores.shape, 0)
        k_at = lax.broadcasted_iota(jnp.int32, scores.shape, 1)
        q_span = scol_ref[first : first + block, :]
        seen = (k_at <= q_at) | ((q_span == srow_ref[:, :last]) & (q_span > 0))
        scores = jnp.where(seen, scores, MASKED)
        raised = jnp.exp(scores - jnp.max(scores, axis=1, keepdims=True))
        probs = (raised / jnp.sum(raised, axis=1, keepdims=True)).astype(BF)
        mixed_ref[first : first + block, :] = dot_nn(probs, vo_ref[:last, :]).astype(BF)


def attend(qkv, inv_q, inv_k, gain_q, gain_k, cosine, sine, span_row, span_col):
    rows = qkv.shape[0]
    width = qkv.shape[1] // 3
    heads = width // HD
    head = lambda shift: pl.BlockSpec((rows, HD), lambda h: (0, h + shift * heads))
    whole = lambda shape: pl.BlockSpec(shape, lambda h: (0, 0))
    out = jax.ShapeDtypeStruct((rows, width), BF)
    return pl.pallas_call(
        functools.partial(attend_kernel, 1.0 / math.sqrt(HD), min(256, rows)),
        grid=(heads,),
        in_specs=[
            head(0), head(1), head(2), whole((rows, 1)), whole((rows, 1)),
            pl.BlockSpec((1, HD), lambda h: (0, h)), pl.BlockSpec((1, HD), lambda h: (0, h)),
            whole((rows, HD)), whole((rows, HD)), whole((1, rows)), whole((rows, 1)),
        ],
        out_specs=[head(0)] * 4,
        out_shape=[out] * 4,
        compiler_params=pltpu.CompilerParams(vmem_limit_bytes=VMEM_LIMIT),
        cost_estimate=pl.CostEstimate(
            flops=4 * rows * rows * width, bytes_accessed=20 * rows * width,
            transcendentals=rows * rows * heads,
        ),
        name="attend",
    )(qkv, qkv, qkv, inv_q, inv_k, gain_q, gain_k, cosine, sine, span_row, span_col)


def attend_back_kernel(
    scale, block, q_ref, k_ref, v_ref, d_ref, cos_ref, sin_ref, srow_ref, scol_ref,
    dq_ref, dk_ref, dv_ref, dk_sum, dv_sum
):
    rows = q_ref.shape[0]
    dk_sum[...] = jnp.zeros_like(dk_sum)
    dv_sum[...] = jnp.zeros_like(dv_sum)

    def turned(values, at):
        return values * cos_ref[at, :] - pltpu.roll(values, HD // 2, 1) * sin_ref[at, :]

    for first in range(0, rows, block):
        here = slice(first, first + block)
        last = min(rows, first + block + IMG)
        queries, keys, grads = q_ref[here, :], k_ref[:last, :], d_ref[here, :]
        scores = dot_nt(keys, queries) * scale
        k_at = lax.broadcasted_iota(jnp.int32, scores.shape, 0)
        q_at = first + lax.broadcasted_iota(jnp.int32, scores.shape, 1)
        q_span = srow_ref[:, here]
        seen = (k_at <= q_at) | ((q_span == scol_ref[:last, :]) & (q_span > 0))
        scores = jnp.where(seen, scores, MASKED)
        raised = jnp.exp(scores - jnp.max(scores, axis=0, keepdims=True))
        probs = raised / jnp.sum(raised, axis=0, keepdims=True)
        d_probs = dot_nt(v_ref[:last, :], grads)
        d_scores = (probs * (d_probs - jnp.sum(probs * d_probs, axis=0, keepdims=True))).astype(BF)
        dq_ref[here, :] = turned(dot_tn(d_scores, keys) * scale, here)
        dk_sum[:last, :] += dot_nn(d_scores, queries)
        dv_sum[:last, :] += dot_nn(probs.astype(BF), grads)
    dk_ref[...] = turned(dk_sum[...] * scale, slice(0, rows))
    dv_ref[...] = dv_sum[...].astype(BF)


def attend_back(queries, keys, values, grads, cosine, sine, span_row, span_col):
    rows, width = queries.shape
    heads = width // HD
    head = pl.BlockSpec((rows, HD), lambda h: (0, h))
    whole = lambda shape: pl.BlockSpec(shape, lambda h: (0, 0))
    return pl.pallas_call(
        functools.partial(attend_back_kernel, 1.0 / math.sqrt(HD), min(256, rows)),
        grid=(heads,),
        in_specs=[head] * 4
        + [whole((rows, HD)), whole((rows, HD)), whole((1, rows)), whole((rows, 1))],
        out_specs=[head] * 3,
        out_shape=[
            jax.ShapeDtypeStruct((rows, width), F32),
            jax.ShapeDtypeStruct((rows, width), F32),
            jax.ShapeDtypeStruct((rows, width), BF),
        ],
        scratch_shapes=[pltpu.VMEM((rows, HD), F32)] * 2,
        compiler_params=pltpu.CompilerParams(vmem_limit_bytes=VMEM_LIMIT),
        cost_estimate=pl.CostEstimate(
            flops=10 * rows * rows * width, bytes_accessed=20 * rows * width,
            transcendentals=rows * rows * heads,
        ),
        name="attend_back",
    )(queries, keys, values, grads, cosine, sine, span_row, span_col)


def moe_kernel(
    first, n_col, closing, x_ref, xt_ref, y_ref, yt_ref, gates_ref, w_ref, *rest
):
    if closing:
        probs_ref, before_ref, router_ref, *rest = rest
    dx_ref, dw_ref, hid_ref, dg_ref, acc, pre, up, grad, d_pre, d_up = rest
    step = pl.program_id(0)
    expert = step + first
    rows, width = x_ref.shape
    n_row, _, _, depth, units = w_ref.shape
    experts = gates_ref.shape[1]

    @pl.when(step == 0)
    def _():
        acc[...] = jnp.zeros_like(acc)
        dg_ref[...] = before_ref[...] if closing else jnp.zeros_like(dg_ref)

    w_gate = w_ref[:, 0, 0].reshape(width, units)
    w_up = w_ref[:, 0, 1].reshape(width, units)
    w_down = w_ref[:, 0, 2].reshape(width, units)
    pre[...] = dot_nn(x_ref[...], w_gate)
    up[...] = dot_nn(x_ref[...], w_up)
    grad[...] = dot_nn(y_ref[...], w_down)

    span = 32

    def activate(i, carry):
        at = pl.ds(pl.multiple_of(i * span, span), span)
        g, u, dh = pre[at, :], up[at, :], grad[at, :]
        mine = lax.broadcasted_iota(jnp.int32, (span, experts), 1) == expert
        gate = jnp.sum(jnp.where(mine, gates_ref[at, :], 0.0), axis=1, keepdims=True)
        s = 1.0 / (1.0 + jnp.exp(-g))
        silu = g * s
        both = silu * u
        hid_ref[0, at, :] = (gate * both).astype(BF)
        d_gate = jnp.sum(dh * both, axis=1, keepdims=True)
        dg_ref[at, :] += jnp.where(mine, d_gate, 0.0)
        act = dh * gate
        d_pre[at, :] = (act * u * (s * (1.0 + g * (1.0 - s)))).astype(BF)
        d_up[at, :] = (act * silu).astype(BF)
        return carry

    lax.fori_loop(0, rows // span, activate, 0)

    dw_ref[:, 0, 0] = dot_nn(xt_ref[...], d_pre[...]).astype(BF).reshape(n_row, depth, units)
    dw_ref[:, 0, 1] = dot_nn(xt_ref[...], d_up[...]).astype(BF).reshape(n_row, depth, units)
    dw_ref[:, 0, 2] = dot_nn(yt_ref[...], hid_ref[0]).astype(BF).reshape(n_row, depth, units)
    part = width // n_col
    for s in range(n_col):
        cols = slice(s * part, (s + 1) * part)
        acc[:, cols] += dot_nt(d_pre[...], w_gate[cols, :]) + dot_nt(d_up[...], w_up[cols, :])

    @pl.when(step == pl.num_programs(0) - 1)
    def _():
        if closing:
            probs = probs_ref[...]
            g = jnp.where(gates_ref[...] > 0.0, dg_ref[...], 0.0)
            low = (probs * (g - jnp.sum(probs * g, axis=1, keepdims=True))).astype(BF)
        for s in range(n_col):
            cols = slice(s * part, (s + 1) * part)
            total = acc[:, cols]
            if closing:
                total = total + dot_nn(low, router_ref[:, cols])
            dx_ref[s] = total.astype(BF)


def moe_half(first, x, xt, y, yt, gates, weights, closing):
    rows, width = x.shape
    n_row, here, _, depth, units = weights.shape
    experts = gates.shape[1]
    n_col = lax.axis_size("col")
    once = lambda shape: pl.BlockSpec(
        shape, lambda e: (0,) * len(shape), pipeline_mode=pl.Buffered(1)
    )
    block = pl.BlockSpec((n_row, 1, 3, depth, units), lambda e: (0, e, 0, 0, 0))
    operands = [x, xt, y, yt, gates, weights]
    in_specs = [
        once((rows, width)), once((width, rows)), once((rows, width)), once((width, rows)),
        once((rows, experts)), block,
    ]
    if closing is not None:
        operands += list(closing)
        in_specs += [once(a.shape) for a in closing]
    return pl.pallas_call(
        functools.partial(moe_kernel, first, n_col, closing is not None),
        grid=(here,),
        in_specs=in_specs,
        out_specs=[
            once((n_col, rows, width // n_col)), block,
            pl.BlockSpec((1, rows, units), lambda e: (e, 0, 0)), once((rows, experts)),
        ],
        out_shape=[
            jax.ShapeDtypeStruct((n_col, rows, width // n_col), BF),
            jax.ShapeDtypeStruct(weights.shape, BF),
            jax.ShapeDtypeStruct((here, rows, units), BF),
            jax.ShapeDtypeStruct((rows, experts), F32),
        ],
        scratch_shapes=[pltpu.VMEM((rows, width), F32)]
        + [pltpu.VMEM((rows, units), F32)] * 3
        + [pltpu.VMEM((rows, units), BF)] * 2,
        compiler_params=pltpu.CompilerParams(vmem_limit_bytes=VMEM_LIMIT),
        cost_estimate=pl.CostEstimate(
            flops=16 * here * rows * width * units,
            bytes_accessed=12 * here * n_row * depth * units + 12 * rows * width,
            transcendentals=here * rows * units,
        ),
        name="experts",
    )(*operands)


def down_kernel(n_col, hid_a, hid_b, w_a, w_b, out_ref, acc):
    step = pl.program_id(0)
    half = pl.num_programs(0) // 2
    rows, width = acc.shape
    part = width // n_col

    @pl.when(step == 0)
    def _():
        acc[...] = jnp.zeros_like(acc)

    def add(hid, weight):
        w_down = weight[:, 0, 0].reshape(width, weight.shape[-1])
        for s in range(n_col):
            cols = slice(s * part, (s + 1) * part)
            acc[:, cols] += dot_nt(hid[0], w_down[cols, :])

    pl.when(step < half)(lambda: add(hid_a, w_a))
    pl.when(step >= half)(lambda: add(hid_b, w_b))

    @pl.when(step == 2 * half - 1)
    def _():
        for s in range(n_col):
            out_ref[s] = acc[:, s * part : (s + 1) * part].astype(BF)


def down(hid_a, hid_b, weights_a, weights_b):
    half, rows, units = hid_a.shape
    n_row, _, _, depth, _ = weights_a.shape
    width = n_row * depth
    n_col = lax.axis_size("col")
    low = lambda e: jnp.minimum(e, half - 1)
    high = lambda e: jnp.maximum(e - half, 0)
    return pl.pallas_call(
        functools.partial(down_kernel, n_col),
        grid=(2 * half,),
        in_specs=[
            pl.BlockSpec((1, rows, units), lambda e: (low(e), 0, 0)),
            pl.BlockSpec((1, rows, units), lambda e: (high(e), 0, 0)),
            pl.BlockSpec((n_row, 1, 1, depth, units), lambda e: (0, low(e), 2, 0, 0)),
            pl.BlockSpec((n_row, 1, 1, depth, units), lambda e: (0, high(e), 2, 0, 0)),
        ],
        out_specs=pl.BlockSpec((n_col, rows, width // n_col), lambda e: (0, 0, 0)),
        out_shape=jax.ShapeDtypeStruct((n_col, rows, width // n_col), BF),
        scratch_shapes=[pltpu.VMEM((rows, width), F32)],
        compiler_params=pltpu.CompilerParams(vmem_limit_bytes=VMEM_LIMIT),
        cost_estimate=pl.CostEstimate(
            flops=4 * half * rows * width * units,
            bytes_accessed=4 * half * (width + rows) * units + 2 * rows * width,
            transcendentals=0,
        ),
        name="down",
    )(hid_a, hid_b, weights_a, weights_b)


def pack_experts(w_gate, w_up, w_down, first, last):
    pick = lambda w: jnp.transpose(w[:, first:last], (1, 0, 2))
    return row_major(jnp.stack([pick(w_gate), pick(w_up), pick(w_down)], axis=1))


def shards(
    tokens, norm_attn, norm_query, norm_key, norm_moe, w_query, w_key, w_value, w_out, w_router,
    w_gate, w_up, w_down, routes, span_starts, cotangent,
):
    rows, part = tokens.shape
    n_col = lax.axis_size("col")
    me = lax.axis_index("col")
    width = part * n_col
    experts = w_gate.shape[1]
    half = experts // 2
    cols = w_router.shape[1]

    pad = (-(4 * part + cols)) % 128
    mats = jnp.concatenate(
        [w_query, w_key, w_value, w_out, w_router, jnp.zeros((w_router.shape[0], pad), BF)], axis=1
    )
    mats = lax.all_gather(mats, "row", axis=0, tiled=True)
    full_qkv = mats[:, : 3 * part]
    full_out = mats[:, 3 * part : 4 * part]
    first_half = lax.all_gather(pack_experts(w_gate, w_up, w_down, 0, half), "row", axis=0)
    second_half = lax.all_gather(pack_experts(w_gate, w_up, w_down, half, experts), "row", axis=0)

    below = jnp.broadcast_to(norm_attn.reshape(1, part), (16, part))
    spread = gather_line(jnp.concatenate([tokens, below], axis=0))
    token_values = jnp.transpose(spread[:, :rows], (1, 0, 2)).reshape(rows, width).astype(F32)
    attn_gain = spread[:, rows].reshape(1, width).astype(F32)
    inv_first = lax.rsqrt(jnp.mean(token_values * token_values, axis=1, keepdims=True) + EPSILON)
    normed_attn = (token_values * inv_first * attn_gain).astype(BF)
    grad_blocks = gather_line(after(cotangent, spread))
    qkv = dot_nn(normed_attn, full_qkv)
    query_raw, key_raw = qkv[:, :part], qkv[:, part : 2 * part]

    squares = sum_small(
        jnp.stack([jnp.sum(query_raw * query_raw, axis=1), jnp.sum(key_raw * key_raw, axis=1)])
    )
    inv_qk = lax.rsqrt(squares / width + EPSILON)
    query_inv, key_inv = inv_qk[0][:, None], inv_qk[1][:, None]
    query_gain, key_gain = norm_query.reshape(1, part), norm_key.reshape(1, part)
    cosine, sine = rope_tables(rows)
    span_of = span_ids(span_starts[0], rows)
    span_row, span_col = span_of[None, :], span_of[:, None]
    queries, keys, values, mixed = attend(
        qkv, query_inv, key_inv, query_gain, key_gain, cosine, sine, span_row, span_col
    )

    attn_parts = dot_nt(mixed, full_out)
    attn = scatter_line(
        lambda s: lax.dynamic_slice_in_dim(attn_parts, s * part, part, 1)
    )
    local_tokens = tokens.astype(F32)
    hidden_state = local_tokens + after(attn, grad_blocks)
    moe_gain = norm_moe.astype(F32).reshape(1, part)
    hidden_square = sum_small(jnp.sum(hidden_state * hidden_state, axis=1)[None])
    inv_second = lax.rsqrt(hidden_square[0][:, None] / width + EPSILON)
    flat = lambda blocks: jnp.transpose(blocks, (1, 0, 2)).reshape(rows, width)
    turn = lambda blocks: jnp.transpose(blocks, (0, 2, 1)).reshape(width, rows)
    moe_blocks = gather_line((hidden_state * inv_second * moe_gain).astype(BF))
    normed_moe, normed_moe_t = flat(moe_blocks), turn(moe_blocks)
    grad_full, grad_full_t = flat(grad_blocks), turn(grad_blocks)

    router_t = gather_small(mats[:, 4 * part : 4 * part + cols].T).reshape(experts, width)
    router_probs = jax.nn.softmax(dot_nt(normed_moe, router_t), axis=1)
    expert_ids = jnp.arange(experts, dtype=jnp.int32)
    routed = jnp.any(routes[:, :, None] == expert_ids[None, None, :], axis=1)
    gate_table = jnp.where(routed, router_probs, 0.0)

    dx_a, dw_a, hid_a, dg_a = moe_half(
        0, normed_moe, normed_moe_t, grad_full, grad_full_t, gate_table, first_half, None
    )
    dx_b, dw_b, hid_b, dg_b = moe_half(
        half, normed_moe, normed_moe_t, grad_full, grad_full_t, gate_table, second_half,
        (router_probs, dg_a, router_t),
    )
    summed_a = lax.psum_scatter(dw_a, "row", scatter_dimension=0)
    summed_b = lax.psum_scatter(dw_b, "row", scatter_dimension=0)

    pick = lambda blocks, s: lax.dynamic_index_in_dim(blocks, s, 0, keepdims=False).astype(F32)
    dx_b = after(dx_b, summed_a)
    moe_in_grad = scatter_line(lambda s: pick(dx_a, s) + pick(dx_b, s))
    moe_stat = sum_small(jnp.sum(moe_in_grad * moe_gain * hidden_state, axis=1)[None])[0][:, None]
    d_moe_gain = jnp.sum(moe_in_grad * hidden_state * inv_second, axis=0)
    hidden_grad = (
        cotangent.astype(F32)
        + inv_second * moe_gain * moe_in_grad
        - inv_second**3 * hidden_state * moe_stat / width
    )
    attn_grad = flat(gather_line(hidden_grad.astype(BF)))
    mixed_grad = dot_nn(attn_grad, full_out).astype(BF)
    d_out_w = dot_tn(attn_grad, mixed)

    query_turned, key_turned, value_grad = attend_back(
        queries, keys, values, after(mixed_grad, summed_b), cosine, sine, span_row, span_col
    )
    query_scaled = query_turned * query_gain.astype(F32)
    key_scaled = key_turned * key_gain.astype(F32)
    stats = sum_small(
        jnp.stack(
            [jnp.sum(query_scaled * query_raw, axis=1), jnp.sum(key_scaled * key_raw, axis=1)]
        )
    )
    d_query_gain = jnp.sum(query_turned * query_raw * query_inv, axis=0)
    d_key_gain = jnp.sum(key_turned * key_raw * key_inv, axis=0)
    query_raw_grad = (
        query_inv * query_scaled - query_inv**3 * query_raw * stats[0][:, None] / width
    ).astype(BF)
    key_raw_grad = (
        key_inv * key_scaled - key_inv**3 * key_raw * stats[1][:, None] / width
    ).astype(BF)
    qkv_grad = jnp.concatenate([query_raw_grad, key_raw_grad, value_grad], axis=1)
    attn_in_terms = dot_nt(qkv_grad, full_qkv)
    d_qkv_w = dot_tn(normed_attn, qkv_grad)

    gate_grad = jnp.where(routed, sum_small(dg_b.T).T, 0.0)
    logit_low = (
        router_probs * (gate_grad - jnp.sum(router_probs * gate_grad, axis=1, keepdims=True))
    ).astype(BF)
    d_router_w = dot_tn(normed_moe, lax.dynamic_slice_in_dim(logit_low, me * cols, cols, 1))

    d_out_mats = jnp.concatenate(
        [d_out_w.astype(BF), d_router_w.astype(BF), jnp.zeros((width, -cols % 128), BF)], axis=1
    )
    summed_out = lax.psum_scatter(
        after(row_major(d_out_mats), summed_b), "row", scatter_dimension=0, tiled=True
    ).astype(F32)
    summed_qkv = lax.psum_scatter(
        after(row_major(d_qkv_w.astype(BF)), summed_out), "row", scatter_dimension=0, tiled=True
    ).astype(F32)

    attn_in_grad = scatter_line(
        lambda s: lax.dynamic_slice_in_dim(attn_in_terms, s * part, part, 1)
    )
    local_gain = norm_attn.astype(F32).reshape(1, part)
    attn_stat = sum_small(jnp.sum(attn_in_grad * local_gain * local_tokens, axis=1)[None])
    d_attn_gain = jnp.sum(attn_in_grad * local_tokens * inv_first, axis=0)
    d_tokens = (
        hidden_grad
        + inv_first * local_gain * attn_in_grad
        - inv_first**3 * local_tokens * attn_stat[0][:, None] / width
    )

    moe_parts = down(hid_a, hid_b, first_half, second_half)
    output = (hidden_state + scatter_line(lambda s: pick(moe_parts, s))).astype(BF)

    gains = lax.psum(jnp.stack([d_attn_gain, d_query_gain, d_key_gain, d_moe_gain]), "row")
    expert_grads = jnp.concatenate([summed_a, summed_b], axis=0)
    unpack = lambda i: jnp.transpose(expert_grads[:, i], (1, 0, 2)).astype(F32)
    cut = lambda i: summed_qkv[:, i * part : (i + 1) * part]
    return (
        output, d_tokens, gains[0], gains[1], gains[2], gains[3],
        cut(0), cut(1), cut(2), summed_out[:, :part], summed_out[:, part : part + cols],
        unpack(0), unpack(1), unpack(2),
    )


def solution(mesh):
    grid = P("row", "col")
    cube = P("row", None, "col")
    rows = P("row", None)
    line = P("col")
    in_specs = (
        grid, line, line, line, line, grid, grid, grid, grid, grid,
        cube, cube, cube, rows, rows, grid,
    )
    out_specs = (
        grid, grid, line, line, line, line, grid, grid, grid, grid, grid, cube, cube, cube,
    )
    return jax.shard_map(shards, mesh=mesh, in_specs=in_specs, out_specs=out_specs, check_vma=False)
```

```python
import functools
import math

import jax
import jax.numpy as jnp
from jax import lax
from jax.experimental import pallas as pl
from jax.experimental.layout import Layout, with_layout_constraint
from jax.experimental.pallas import tpu as pltpu
from jax.sharding import PartitionSpec as P

HD = 128
IMG = 256

EPSILON = 1e-05
ROPE_BASE = 10000.0
MASKED = -1e30
VMEM_LIMIT = 66_000_000
BF = jnp.bfloat16
F32 = jnp.float32


def dot_nn(a, b):
    return lax.dot_general(a, b, (((1,), (0,)), ((), ())), preferred_element_type=F32)


def dot_nt(a, b):
    return lax.dot_general(a, b, (((1,), (1,)), ((), ())), preferred_element_type=F32)


def dot_tn(a, b):
    return lax.dot_general(a, b, (((0,), (0,)), ((), ())), preferred_element_type=F32)


def row_major(values):
    return with_layout_constraint(values, Layout(major_to_minor=tuple(range(values.ndim))))


def zero_of(values):
    return jnp.minimum(jnp.abs(values[(0,) * values.ndim].astype(F32)), 0.0).astype(BF)


def shift(values, k):
    n = lax.axis_size("col")
    return lax.ppermute(values, "col", [(i, (i + k) % n) for i in range(n)])


def pieces_line(block):
    n = lax.axis_size("col")
    far = {k: shift(block, k) for k in (*range(2, n), 1)}
    return [far[k] for k in range(1, n)]


def scatter_line(part):
    n = lax.axis_size("col")
    me = lax.axis_index("col")
    others = [
        shift(part(lax.rem(me + k, n)).astype(BF), k) for k in (*range(2, n), 1)
    ]
    total = part(me).astype(F32)
    return total, others


def sum_small(values):
    n = lax.axis_size("col")
    total = values
    for k in range(1, n):
        total = total + lax.ppermute(values, "col", [(i, (i + k) % n) for i in range(n)])
    return total


def gather_small(values):
    n = lax.axis_size("col")
    me = lax.axis_index("col")
    out = jnp.zeros((n, *values.shape), values.dtype)
    out = lax.dynamic_update_index_in_dim(out, values, me, 0)
    for k in range(1, n):
        piece = lax.ppermute(values, "col", [(i, (i + k) % n) for i in range(n)])
        out = lax.dynamic_update_index_in_dim(out, piece, lax.rem(me - k + n, n), 0)
    return out


CHUNK = 128


def line_kernel(n, make, n_in, n_out, *refs):
    plan = make(refs[:n_in], refs[n_in : n_in + n_out])
    term, first, second, out = plan
    stat_out, stat_in, stat_sem, *rest = refs[n_in + n_out :]
    if term is not None:
        sums, held, sum_sem, *rest = rest
    if out is not None:
        (gather_sem,) = rest
    chunks = stat_out.shape[0]
    me = lax.axis_index("col")
    ways = ((1, me > 0, me < n - 1), (-1, me < n - 1, me > 0))

    barrier = pltpu.get_barrier_semaphore()
    for k in range(1, n):
        pl.semaphore_signal(
            barrier, inc=1, device_id={"col": lax.rem(me + k, n)},
            device_id_type=pl.DeviceIdType.MESH,
        )
    pl.semaphore_wait(barrier, n - 1)

    def at(c):
        return pl.ds(pl.multiple_of(c * CHUNK, CHUNK), CHUNK)

    def remote(ref, sems, index, other):
        return pltpu.make_async_remote_copy(
            src_ref=ref, dst_ref=ref, send_sem=sems.at[(0, *index)], recv_sem=sems.at[(1, *index)],
            device_id={"col": other}, device_id_type=pl.DeviceIdType.MESH,
        )

    def sum_copy(way, s, c, other):
        return remote(sums.at[way, s, at(c)], sum_sem, (way, s, c), other)

    def gather_copy(way, s, c, other):
        part = out.shape[1] // n
        block = out.at[at(c), pl.ds(pl.multiple_of(s * part, part), part)]
        return remote(block, gather_sem, (way, s, c), other)

    def stat_copy(k, c):
        return pltpu.make_async_remote_copy(
            src_ref=stat_out.at[c], dst_ref=stat_in.at[k, c], send_sem=stat_sem.at[0, k, c],
            recv_sem=stat_sem.at[1, k, c], device_id={"col": lax.rem(me + k, n)},
            device_id_type=pl.DeviceIdType.MESH,
        )

    def arrived(way, s, c):
        step, has_source, _ = ways[way]

        @pl.when(has_source)
        def _():
            sum_copy(way, s, c, me - step).wait_recv()

        @pl.when(jnp.logical_not(has_source))
        def _():
            sums[way, s, at(c)] = jnp.zeros_like(sums[way, s, at(c)])

    depths = (me, n - 1 - me)
    hops = []
    for j in range(n - 1):
        hops += [(0, n - 1 - j, n - 1 - j > me), (1, j, j < me)]

    def on_turn(t, hop, action):
        way, s, mine = hop
        c = t - depths[way]
        pl.when(mine & (c >= 0) & (c < chunks))(lambda: action(way, s, c))

    def ready(way, s, c):
        held[way] = term(at(c), s)

    def add(way, s, c):
        arrived(way, s, c)
        sums[way, s, at(c)] = (held[way] + sums[way, s, at(c)].astype(F32)).astype(BF)

    def send(way, s, c):
        sum_copy(way, s, c, me + ways[way][0]).start()

    def finish(c):
        total = None
        if term is not None:
            arrived(0, me, c)
            arrived(1, me, c)
            total = (
                term(at(c), me) + sums[0, me, at(c)].astype(F32) + sums[1, me, at(c)].astype(F32)
            )
        stat = jnp.broadcast_to(first(at(c), total), (CHUNK, 128))
        stat_out[c] = stat.T[:8]

    def apply(c):
        row = stat_out[c]
        for k in range(1, n):
            stat_copy(k, c).wait_recv()
            row = row + stat_in[k, c]
        stat = jnp.broadcast_to(row[:1], (128, CHUNK)).T[:, :1]
        block = second(at(c), stat)
        if out is not None:
            part = out.shape[1] // n
            out[at(c), pl.ds(pl.multiple_of(me * part, part), part)] = block

    def pass_on(c, r):
        for way, (step, _, has_target) in enumerate(ways):
            s = me - step * r
            there = jnp.logical_and(s >= 0, s < n)
            if r > 0:
                @pl.when(there)
                def _():
                    gather_copy(way, s, c, me - step).wait_recv()

            @pl.when(jnp.logical_and(there, has_target))
            def _():
                gather_copy(way, s, c, me + step).start()

    lag = 0 if term is None else n - 1
    last = lag + 1 + (0 if out is None else n)

    def body(t, carry):
        def stage(delay, action):
            c = t - delay
            pl.when(jnp.logical_and(c >= 0, c < chunks))(lambda: action(c))

        if out is not None:
            for r in range(n - 1, -1, -1):
                stage(lag + 2 + r, lambda c: pass_on(c, r))
        if term is not None:
            on_turn(t, hops[0], ready)
            for hop, later in zip(hops, hops[1:]):
                on_turn(t, hop, add)
                on_turn(t, later, ready)
                on_turn(t, hop, send)
            on_turn(t, hops[-1], add)
        stage(lag, finish)
        if term is not None:
            on_turn(t, hops[-1], send)
        stage(lag + 1, apply)

        def tell(c):
            for k in range(1, n):
                stat_copy(k, c).start()

        stage(lag, tell)
        return carry

    lax.fori_loop(0, chunks + last + 1, body, 0)

    def drain(c, carry):
        for k in range(1, n):
            stat_copy(k, c).wait_send()
        if term is not None:
            for way, s, mine in hops:
                @pl.when(mine)
                def _():
                    sum_copy(way, s, c, me + ways[way][0]).wait_send()
        if out is not None:
            for r in range(n):
                for way, (step, _, has_target) in enumerate(ways):
                    s = me - step * r
                    there = jnp.logical_and(s >= 0, s < n)

                    @pl.when(jnp.logical_and(there, has_target))
                    def _():
                        gather_copy(way, s, c, me + step).wait_send()
        return carry

    lax.fori_loop(0, chunks, drain, 0)


def along_line(make, operands, out_shape, rows, part, sums, gathers, number, name, others=()):
    n = lax.axis_size("col")
    chunks = rows // CHUNK
    vmem = pl.BlockSpec(memory_space=pltpu.VMEM)
    scratch = [
        pltpu.VMEM((chunks, 8, 128), F32), pltpu.VMEM((n, chunks, 8, 128), F32),
        pltpu.SemaphoreType.DMA((2, n, chunks)),
    ]
    if sums:
        scratch += [
            pltpu.VMEM((2, n, rows, part), BF), pltpu.VMEM((2, CHUNK, part), F32),
            pltpu.SemaphoreType.DMA((2, 2, n, chunks)),
        ]
    if gathers:
        scratch += [pltpu.SemaphoreType.DMA((2, 2, n, chunks))]
    return pl.pallas_call(
        functools.partial(line_kernel, n, make, len(operands), len(out_shape)),
        in_specs=[vmem] * (len(operands) - len(others)) + list(others),
        out_specs=[vmem] * len(out_shape),
        out_shape=out_shape,
        scratch_shapes=scratch,
        compiler_params=pltpu.CompilerParams(
            vmem_limit_bytes=VMEM_LIMIT, collective_id=number, has_side_effects=True
        ),
        cost_estimate=pl.CostEstimate(
            flops=1_000_000, bytes_accessed=rows * part, transcendentals=0
        ),
        name=name,
    )(*operands)


def norm_line(tokens, gain, width):
    rows, part = tokens.shape

    def make(ins, outs):
        x_ref, gain_ref = ins
        out_ref, inv_ref = outs

        def first(at, total):
            x = x_ref[at, :].astype(F32)
            return jnp.sum(x * x, axis=1, keepdims=True)

        def second(at, stat):
            inv = lax.rsqrt(stat / width + EPSILON)
            inv_ref[at, :] = inv
            return (x_ref[at, :].astype(F32) * inv * gain_ref[...].astype(F32)).astype(BF)

        return None, first, second, out_ref

    out_shape = [
        jax.ShapeDtypeStruct((rows, width), BF), jax.ShapeDtypeStruct((rows, 1), F32)
    ]
    return along_line(make, [tokens, gain], out_shape, rows, part, False, True, 1, "norm_line")


def attn_line(mixed, w_out, tokens, gain, width):
    rows, part = tokens.shape

    def make(ins, outs):
        m_ref, w_ref, x_ref, gain_ref = ins
        out_ref, hidden_ref, inv_ref = outs

        def term(at, s):
            return dot_nt(m_ref[at, :], w_ref[pl.ds(s * part, part), :])

        def first(at, total):
            hidden = x_ref[at, :].astype(F32) + total
            hidden_ref[at, :] = hidden
            return jnp.sum(hidden * hidden, axis=1, keepdims=True)

        def second(at, stat):
            inv = lax.rsqrt(stat / width + EPSILON)
            inv_ref[at, :] = inv
            return (hidden_ref[at, :] * inv * gain_ref[...].astype(F32)).astype(BF)

        return term, first, second, out_ref

    out_shape = [
        jax.ShapeDtypeStruct((rows, width), BF), jax.ShapeDtypeStruct((rows, part), F32),
        jax.ShapeDtypeStruct((rows, 1), F32),
    ]
    return along_line(
        make, [mixed, w_out, tokens, gain], out_shape, rows, part, True, True, 2, "attn_line"
    )


def moe_line(terms, hidden, inv, gain, grads, earlier, width):
    rows, part = hidden.shape

    def make(ins, outs):
        t_ref, hidden_ref, inv_ref, gain_ref, y_ref, _ = ins
        out_ref, grad_ref, d_gain_ref = outs
        d_gain_ref[...] = jnp.zeros_like(d_gain_ref)

        def term(at, s):
            return t_ref[s, at, :].astype(F32)

        def first(at, total):
            grad_ref[at, :] = total
            product = total * hidden_ref[at, :]
            d_gain_ref[...] += jnp.sum(product * inv_ref[at, :], axis=0, keepdims=True)
            return jnp.sum(product * gain_ref[...].astype(F32), axis=1, keepdims=True)

        def second(at, stat):
            factor = inv_ref[at, :]
            grad = (
                y_ref[at, :].astype(F32)
                + factor * gain_ref[...].astype(F32) * grad_ref[at, :]
                - factor * factor * factor * (stat / width) * hidden_ref[at, :]
            )
            grad_ref[at, :] = grad
            return grad.astype(BF)

        return term, first, second, out_ref

    out_shape = [
        jax.ShapeDtypeStruct((rows, width), BF), jax.ShapeDtypeStruct((rows, part), F32),
        jax.ShapeDtypeStruct((1, part), F32),
    ]
    return along_line(
        make, [terms, hidden, inv, gain, grads, earlier], out_shape, rows, part, True, True, 3,
        "moe_line", [pl.BlockSpec(memory_space=pl.ANY)],
    )


def input_line(qkv_grad, w_qkv, tokens, inv, gain, grads, width):
    rows, part = tokens.shape

    def make(ins, outs):
        q_ref, w_ref, x_ref, inv_ref, gain_ref, y_ref = ins
        grad_ref, d_gain_ref = outs
        d_gain_ref[...] = jnp.zeros_like(d_gain_ref)

        def term(at, s):
            return dot_nt(q_ref[at, :], w_ref[pl.ds(s * part, part), :])

        def first(at, total):
            grad_ref[at, :] = total
            product = total * x_ref[at, :].astype(F32)
            d_gain_ref[...] += jnp.sum(product * inv_ref[at, :], axis=0, keepdims=True)
            return jnp.sum(product * gain_ref[...].astype(F32), axis=1, keepdims=True)

        def second(at, stat):
            factor = inv_ref[at, :]
            grad_ref[at, :] = (
                y_ref[at, :]
                + factor * gain_ref[...].astype(F32) * grad_ref[at, :]
                - factor * factor * factor * (stat / width) * x_ref[at, :].astype(F32)
            )

        return term, first, second, None

    out_shape = [jax.ShapeDtypeStruct((rows, part), F32), jax.ShapeDtypeStruct((1, part), F32)]
    return along_line(
        make, [qkv_grad, w_qkv, tokens, inv, gain, grads], out_shape, rows, part, True, False, 4,
        "input_line",
    )


def rope_tables(length):
    half_size = HD // 2
    places = jnp.arange(length, dtype=F32)
    rates = jnp.exp(-math.log(ROPE_BASE) * jnp.arange(half_size, dtype=F32) / half_size)
    angles = places[:, None] * rates[None, :]
    cosine, sine = jnp.cos(angles), jnp.sin(angles)
    return jnp.concatenate([cosine, cosine], 1), jnp.concatenate([-sine, sine], 1)


def span_ids(starts, length):
    places = jnp.arange(length, dtype=jnp.int32)
    inside = (places[None, :] >= starts[:, None]) & (places[None, :] < starts[:, None] + IMG)
    numbers = jnp.arange(1, starts.shape[0] + 1, dtype=jnp.int32)
    return jnp.sum(jnp.where(inside, numbers[:, None], 0), axis=0)


def attend_kernel(
    scale, block, q_ref, k_ref, v_ref, iq_ref, ik_ref, gq_ref, gk_ref, cos_ref, sin_ref,
    srow_ref, scol_ref, qo_ref, ko_ref, vo_ref, mixed_ref
):
    rows = q_ref.shape[0]
    cosine, sine = cos_ref[...], sin_ref[...]

    def turned(raw_ref, inv_ref, gain_ref):
        normed = raw_ref[...] * inv_ref[...] * gain_ref[...].astype(F32)
        return (normed * cosine + pltpu.roll(normed, HD // 2, 1) * sine).astype(BF)

    qo_ref[...] = turned(q_ref, iq_ref, gq_ref)
    ko_ref[...] = turned(k_ref, ik_ref, gk_ref)
    vo_ref[...] = v_ref[...].astype(BF)
    for first in range(0, rows, block):
        last = min(rows, first + block + IMG)
        scores = dot_nt(qo_ref[first : first + block, :], ko_ref[:last, :]) * scale
        q_at = first + lax.broadcasted_iota(jnp.int32, scores.shape, 0)
        k_at = lax.broadcasted_iota(jnp.int32, scores.shape, 1)
        q_span = scol_ref[first : first + block, :]
        seen = (k_at <= q_at) | ((q_span == srow_ref[:, :last]) & (q_span > 0))
        scores = jnp.where(seen, scores, MASKED)
        raised = jnp.exp(scores - jnp.max(scores, axis=1, keepdims=True))
        probs = (raised / jnp.sum(raised, axis=1, keepdims=True)).astype(BF)
        mixed_ref[first : first + block, :] = dot_nn(probs, vo_ref[:last, :]).astype(BF)


def attend(qkv, inv_q, inv_k, gain_q, gain_k, cosine, sine, span_row, span_col):
    rows = qkv.shape[0]
    width = qkv.shape[1] // 3
    heads = width // HD
    head = lambda shift: pl.BlockSpec((rows, HD), lambda h: (0, h + shift * heads))
    whole = lambda shape: pl.BlockSpec(shape, lambda h: (0, 0))
    out = jax.ShapeDtypeStruct((rows, width), BF)
    return pl.pallas_call(
        functools.partial(attend_kernel, 1.0 / math.sqrt(HD), min(256, rows)),
        grid=(heads,),
        in_specs=[
            head(0), head(1), head(2), whole((rows, 1)), whole((rows, 1)),
            pl.BlockSpec((1, HD), lambda h: (0, h)), pl.BlockSpec((1, HD), lambda h: (0, h)),
            whole((rows, HD)), whole((rows, HD)), whole((1, rows)), whole((rows, 1)),
        ],
        out_specs=[head(0)] * 4,
        out_shape=[out] * 4,
        compiler_params=pltpu.CompilerParams(vmem_limit_bytes=VMEM_LIMIT),
        cost_estimate=pl.CostEstimate(
            flops=4 * rows * rows * width, bytes_accessed=20 * rows * width,
            transcendentals=rows * rows * heads,
        ),
        name="attend",
    )(qkv, qkv, qkv, inv_q, inv_k, gain_q, gain_k, cosine, sine, span_row, span_col)


def attend_back_kernel(
    scale, block, q_ref, k_ref, v_ref, d_ref, cos_ref, sin_ref, srow_ref, scol_ref, _,
    dq_ref, dk_ref, dv_ref, dk_sum, dv_sum
):
    rows = q_ref.shape[0]
    dk_sum[...] = jnp.zeros_like(dk_sum)
    dv_sum[...] = jnp.zeros_like(dv_sum)

    def turned(values, at):
        return values * cos_ref[at, :] - pltpu.roll(values, HD // 2, 1) * sin_ref[at, :]

    for first in range(0, rows, block):
        here = slice(first, first + block)
        last = min(rows, first + block + IMG)
        queries, keys, grads = q_ref[here, :], k_ref[:last, :], d_ref[here, :]
        scores = dot_nt(keys, queries) * scale
        k_at = lax.broadcasted_iota(jnp.int32, scores.shape, 0)
        q_at = first + lax.broadcasted_iota(jnp.int32, scores.shape, 1)
        q_span = srow_ref[:, here]
        seen = (k_at <= q_at) | ((q_span == scol_ref[:last, :]) & (q_span > 0))
        scores = jnp.where(seen, scores, MASKED)
        raised = jnp.exp(scores - jnp.max(scores, axis=0, keepdims=True))
        probs = raised / jnp.sum(raised, axis=0, keepdims=True)
        d_probs = dot_nt(v_ref[:last, :], grads)
        d_scores = (probs * (d_probs - jnp.sum(probs * d_probs, axis=0, keepdims=True))).astype(BF)
        dq_ref[here, :] = turned(dot_tn(d_scores, keys) * scale, here)
        dk_sum[:last, :] += dot_nn(d_scores, queries)
        dv_sum[:last, :] += dot_nn(probs.astype(BF), grads)
    dk_ref[...] = turned(dk_sum[...] * scale, slice(0, rows))
    dv_ref[...] = dv_sum[...].astype(BF)


def attend_back(queries, keys, values, grads, cosine, sine, span_row, span_col, earlier):
    rows, width = queries.shape
    heads = width // HD
    head = pl.BlockSpec((rows, HD), lambda h: (0, h))
    whole = lambda shape: pl.BlockSpec(shape, lambda h: (0, 0))
    return pl.pallas_call(
        functools.partial(attend_back_kernel, 1.0 / math.sqrt(HD), min(256, rows)),
        grid=(heads,),
        in_specs=[head] * 4
        + [whole((rows, HD)), whole((rows, HD)), whole((1, rows)), whole((rows, 1))]
        + [pl.BlockSpec(memory_space=pl.ANY)],
        out_specs=[head] * 3,
        out_shape=[
            jax.ShapeDtypeStruct((rows, width), F32),
            jax.ShapeDtypeStruct((rows, width), F32),
            jax.ShapeDtypeStruct((rows, width), BF),
        ],
        scratch_shapes=[pltpu.VMEM((rows, HD), F32)] * 2,
        compiler_params=pltpu.CompilerParams(vmem_limit_bytes=VMEM_LIMIT),
        cost_estimate=pl.CostEstimate(
            flops=10 * rows * rows * width, bytes_accessed=20 * rows * width,
            transcendentals=rows * rows * heads,
        ),
        name="attend_back",
    )(queries, keys, values, grads, cosine, sine, span_row, span_col, earlier)


def prepare_kernel(n, x_ref, own_ref, *refs):
    pieces, (xt_ref, y_ref, yt_ref) = refs[: n - 1], refs[n - 1 :]
    part = own_ref.shape[1]
    me = lax.axis_index("col")
    for s in range(n):
        cols = slice(s * part, (s + 1) * part)
        xt_ref[cols, :] = x_ref[:, cols].T
    for k, piece in enumerate((own_ref, *pieces)):
        cols = pl.ds(pl.multiple_of(lax.rem(me - k + n, n) * part, part), part)
        y_ref[:, cols] = piece[...]
        yt_ref[cols, :] = piece[...].T


def prepare(x, own, pieces):
    rows, width = x.shape
    part = own.shape[1]
    n = width // part
    step = min(256, rows)
    wide = pl.BlockSpec((step, width), lambda i: (i, 0))
    tall = pl.BlockSpec((width, step), lambda i: (0, i))
    block = pl.BlockSpec((step, part), lambda i: (i, 0))
    out = lambda a, b: jax.ShapeDtypeStruct((a, b), BF)
    return pl.pallas_call(
        functools.partial(prepare_kernel, n),
        grid=(rows // step,),
        in_specs=[wide] + [block] * n,
        out_specs=[tall, wide, tall],
        out_shape=[out(width, rows), out(rows, width), out(width, rows)],
        compiler_params=pltpu.CompilerParams(vmem_limit_bytes=VMEM_LIMIT),
        cost_estimate=pl.CostEstimate(
            flops=0, bytes_accessed=10 * rows * width, transcendentals=0
        ),
        name="prepare",
    )(x, own, *pieces)


def moe_kernel(
    first, n_col, closing, x_ref, xt_ref, y_ref, yt_ref, gates_ref, w_ref, *rest
):
    if closing:
        probs_ref, before_ref, router_ref, first_ref, *rest = rest
    dx_ref, dw_ref, hid_ref, dg_ref, acc, pre, up, grad, d_pre, d_up = rest
    step = pl.program_id(0)
    expert = step + first
    rows, width = x_ref.shape
    n_row, _, _, depth, units = w_ref.shape
    experts = gates_ref.shape[1]

    @pl.when(step == 0)
    def _():
        acc[...] = jnp.zeros_like(acc)
        dg_ref[...] = before_ref[...] if closing else jnp.zeros_like(dg_ref)

    w_gate = w_ref[:, 0, 0].reshape(width, units)
    w_up = w_ref[:, 0, 1].reshape(width, units)
    w_down = w_ref[:, 0, 2].reshape(width, units)
    pre[...] = dot_nn(x_ref[...], w_gate)
    up[...] = dot_nn(x_ref[...], w_up)
    grad[...] = dot_nn(y_ref[...], w_down)

    span = 32

    def activate(i, carry):
        at = pl.ds(pl.multiple_of(i * span, span), span)
        g, u, dh = pre[at, :], up[at, :], grad[at, :]
        mine = lax.broadcasted_iota(jnp.int32, (span, experts), 1) == expert
        gate = jnp.sum(jnp.where(mine, gates_ref[at, :], 0.0), axis=1, keepdims=True)
        s = 1.0 / (1.0 + jnp.exp(-g))
        silu = g * s
        both = silu * u
        hid_ref[0, at, :] = (gate * both).astype(BF)
        d_gate = jnp.sum(dh * both, axis=1, keepdims=True)
        dg_ref[at, :] += jnp.where(mine, d_gate, 0.0)
        act = dh * gate
        d_pre[at, :] = (act * u * (s * (1.0 + g * (1.0 - s)))).astype(BF)
        d_up[at, :] = (act * silu).astype(BF)
        return carry

    lax.fori_loop(0, rows // span, activate, 0)

    dw_ref[:, 0, 0] = dot_nn(xt_ref[...], d_pre[...]).astype(BF).reshape(n_row, depth, units)
    dw_ref[:, 0, 1] = dot_nn(xt_ref[...], d_up[...]).astype(BF).reshape(n_row, depth, units)
    dw_ref[:, 0, 2] = dot_nn(yt_ref[...], hid_ref[0]).astype(BF).reshape(n_row, depth, units)
    part = width // n_col
    for s in range(n_col):
        cols = slice(s * part, (s + 1) * part)
        acc[:, cols] += dot_nt(d_pre[...], w_gate[cols, :]) + dot_nt(d_up[...], w_up[cols, :])

    @pl.when(step == pl.num_programs(0) - 1)
    def _():
        if closing:
            probs = probs_ref[...]
            g = jnp.where(gates_ref[...] > 0.0, dg_ref[...], 0.0)
            low = (probs * (g - jnp.sum(probs * g, axis=1, keepdims=True))).astype(BF)
        for s in range(n_col):
            cols = slice(s * part, (s + 1) * part)
            total = acc[:, cols]
            if closing:
                total = total + dot_nn(low, router_ref[:, cols]) + first_ref[s].astype(F32)
            dx_ref[s] = total.astype(BF)


def moe_half(first, x, xt, y, yt, gates, weights, closing):
    rows, width = x.shape
    n_row, here, _, depth, units = weights.shape
    experts = gates.shape[1]
    n_col = lax.axis_size("col")
    once = lambda shape: pl.BlockSpec(
        shape, lambda e: (0,) * len(shape), pipeline_mode=pl.Buffered(1)
    )
    block = pl.BlockSpec((n_row, 1, 3, depth, units), lambda e: (0, e, 0, 0, 0))
    operands = [x, xt, y, yt, gates, weights]
    in_specs = [
        once((rows, width)), once((width, rows)), once((rows, width)), once((width, rows)),
        once((rows, experts)), block,
    ]
    if closing is not None:
        operands += list(closing)
        in_specs += [once(a.shape) for a in closing]
    return pl.pallas_call(
        functools.partial(moe_kernel, first, n_col, closing is not None),
        grid=(here,),
        in_specs=in_specs,
        out_specs=[
            once((n_col, rows, width // n_col)), block,
            pl.BlockSpec((1, rows, units), lambda e: (e, 0, 0)), once((rows, experts)),
        ],
        out_shape=[
            jax.ShapeDtypeStruct((n_col, rows, width // n_col), BF),
            jax.ShapeDtypeStruct(weights.shape, BF),
            jax.ShapeDtypeStruct((here, rows, units), BF),
            jax.ShapeDtypeStruct((rows, experts), F32),
        ],
        scratch_shapes=[pltpu.VMEM((rows, width), F32)]
        + [pltpu.VMEM((rows, units), F32)] * 3
        + [pltpu.VMEM((rows, units), BF)] * 2,
        compiler_params=pltpu.CompilerParams(vmem_limit_bytes=VMEM_LIMIT),
        cost_estimate=pl.CostEstimate(
            flops=16 * here * rows * width * units,
            bytes_accessed=12 * here * n_row * depth * units + 12 * rows * width,
            transcendentals=here * rows * units,
        ),
        name="experts",
    )(*operands)


def down_kernel(n_col, hid_a, hid_b, w_a, w_b, out_ref, acc):
    step = pl.program_id(0)
    half = pl.num_programs(0) // 2
    rows, width = acc.shape
    part = width // n_col

    @pl.when(step == 0)
    def _():
        acc[...] = jnp.zeros_like(acc)

    def add(hid, weight):
        w_down = weight[:, 0, 0].reshape(width, weight.shape[-1])
        for s in range(n_col):
            cols = slice(s * part, (s + 1) * part)
            acc[:, cols] += dot_nt(hid[0], w_down[cols, :])

    pl.when(step < half)(lambda: add(hid_a, w_a))
    pl.when(step >= half)(lambda: add(hid_b, w_b))

    @pl.when(step == 2 * half - 1)
    def _():
        for s in range(n_col):
            out_ref[s] = acc[:, s * part : (s + 1) * part].astype(BF)


def down(hid_a, hid_b, weights_a, weights_b):
    half, rows, units = hid_a.shape
    n_row, _, _, depth, _ = weights_a.shape
    width = n_row * depth
    n_col = lax.axis_size("col")
    low = lambda e: jnp.minimum(e, half - 1)
    high = lambda e: jnp.maximum(e - half, 0)
    return pl.pallas_call(
        functools.partial(down_kernel, n_col),
        grid=(2 * half,),
        in_specs=[
            pl.BlockSpec((1, rows, units), lambda e: (low(e), 0, 0)),
            pl.BlockSpec((1, rows, units), lambda e: (high(e), 0, 0)),
            pl.BlockSpec((n_row, 1, 1, depth, units), lambda e: (0, low(e), 2, 0, 0)),
            pl.BlockSpec((n_row, 1, 1, depth, units), lambda e: (0, high(e), 2, 0, 0)),
        ],
        out_specs=pl.BlockSpec((n_col, rows, width // n_col), lambda e: (0, 0, 0)),
        out_shape=jax.ShapeDtypeStruct((n_col, rows, width // n_col), BF),
        scratch_shapes=[pltpu.VMEM((rows, width), F32)],
        compiler_params=pltpu.CompilerParams(vmem_limit_bytes=VMEM_LIMIT),
        cost_estimate=pl.CostEstimate(
            flops=4 * half * rows * width * units,
            bytes_accessed=4 * half * (width + rows) * units + 2 * rows * width,
            transcendentals=0,
        ),
        name="down",
    )(hid_a, hid_b, weights_a, weights_b)


def pack_experts(w_gate, w_up, w_down, first, last):
    pick = lambda w: jnp.transpose(w[:, first:last], (1, 0, 2))
    return row_major(jnp.stack([pick(w_gate), pick(w_up), pick(w_down)], axis=1))


def shards(
    tokens, norm_attn, norm_query, norm_key, norm_moe, w_query, w_key, w_value, w_out, w_router,
    w_gate, w_up, w_down, routes, span_starts, cotangent,
):
    rows, part = tokens.shape
    n_col = lax.axis_size("col")
    me = lax.axis_index("col")
    width = part * n_col
    experts = w_gate.shape[1]
    half = experts // 2
    cols = w_router.shape[1]

    pad = (-(4 * part + cols)) % 128
    mats = jnp.concatenate(
        [w_query, w_key, w_value, w_out, w_router, jnp.zeros((w_router.shape[0], pad), BF)], axis=1
    )
    mats = lax.all_gather(mats, "row", axis=0, tiled=True)
    full_qkv = mats[:, : 3 * part]
    full_out = mats[:, 3 * part : 4 * part]
    first_half = lax.all_gather(pack_experts(w_gate, w_up, w_down, 0, half), "row", axis=0)
    second_half = lax.all_gather(pack_experts(w_gate, w_up, w_down, half, experts), "row", axis=0)

    attn_gain = norm_attn.reshape(1, part)
    normed_attn, inv_first = norm_line(tokens, attn_gain, width)
    grad_pieces = pieces_line(cotangent + zero_of(normed_attn))
    qkv = dot_nn(normed_attn, full_qkv)
    query_raw, key_raw = qkv[:, :part], qkv[:, part : 2 * part]

    squares = sum_small(
        jnp.stack([jnp.sum(query_raw * query_raw, axis=1), jnp.sum(key_raw * key_raw, axis=1)])
    )
    inv_qk = lax.rsqrt(squares / width + EPSILON)
    query_inv, key_inv = inv_qk[0][:, None], inv_qk[1][:, None]
    query_gain, key_gain = norm_query.reshape(1, part), norm_key.reshape(1, part)
    cosine, sine = rope_tables(rows)
    span_of = span_ids(span_starts[0], rows)
    span_row, span_col = span_of[None, :], span_of[:, None]
    queries, keys, values, mixed = attend(
        qkv, query_inv, key_inv, query_gain, key_gain, cosine, sine, span_row, span_col
    )

    moe_gain = norm_moe.reshape(1, part)
    normed_moe, hidden_state, inv_second = attn_line(mixed, full_out, tokens, moe_gain, width)
    normed_moe_t, grad_full, grad_full_t = prepare(normed_moe, cotangent, grad_pieces)

    router_t = gather_small(mats[:, 4 * part : 4 * part + cols].T).reshape(experts, width)
    router_probs = jax.nn.softmax(dot_nt(normed_moe, router_t), axis=1)
    expert_ids = jnp.arange(experts, dtype=jnp.int32)
    routed = jnp.any(routes[:, :, None] == expert_ids[None, None, :], axis=1)
    gate_table = jnp.where(routed, router_probs, 0.0)

    dx_a, dw_a, hid_a, dg_a = moe_half(
        0, normed_moe, normed_moe_t, grad_full, grad_full_t, gate_table, first_half, None
    )
    dx_b, dw_b, hid_b, dg_b = moe_half(
        half, normed_moe, normed_moe_t, grad_full, grad_full_t, gate_table, second_half,
        (router_probs, dg_a, router_t, dx_a),
    )
    summed_a = lax.psum_scatter(dw_a, "row", scatter_dimension=0)
    summed_b = lax.psum_scatter(dw_b, "row", scatter_dimension=0)
    moe_parts = down(hid_a, hid_b, first_half, second_half)

    attn_grad, hidden_grad, d_moe_gain = moe_line(
        dx_b, hidden_state, inv_second, moe_gain, cotangent, moe_parts, width
    )
    parted = zero_of(attn_grad)
    pick = lambda s: lax.dynamic_index_in_dim(moe_parts, s, 0, keepdims=False) + parted
    own_part, other_parts = scatter_line(pick)
    mixed_grad = dot_nn(attn_grad, full_out).astype(BF)
    d_out_w = dot_tn(attn_grad, mixed)

    query_turned, key_turned, value_grad = attend_back(
        queries, keys, values, mixed_grad, cosine, sine, span_row, span_col, summed_a
    )
    query_scaled = query_turned * query_gain.astype(F32)
    key_scaled = key_turned * key_gain.astype(F32)
    stats = sum_small(
        jnp.stack(
            [jnp.sum(query_scaled * query_raw, axis=1), jnp.sum(key_scaled * key_raw, axis=1)]
        )
    )
    d_query_gain = jnp.sum(query_turned * query_raw * query_inv, axis=0)
    d_key_gain = jnp.sum(key_turned * key_raw * key_inv, axis=0)
    query_raw_grad = (
        query_inv * query_scaled - query_inv**3 * query_raw * stats[0][:, None] / width
    ).astype(BF)
    key_raw_grad = (
        key_inv * key_scaled - key_inv**3 * key_raw * stats[1][:, None] / width
    ).astype(BF)
    qkv_grad = jnp.concatenate([query_raw_grad, key_raw_grad, value_grad], axis=1)
    d_tokens, d_attn_gain = input_line(
        qkv_grad, full_qkv, tokens, inv_first, attn_gain, hidden_grad, width
    )
    d_qkv_w = dot_tn(normed_attn, qkv_grad)

    gate_grad = jnp.where(routed, sum_small(dg_b.T).T, 0.0)
    logit_low = (
        router_probs * (gate_grad - jnp.sum(router_probs * gate_grad, axis=1, keepdims=True))
    ).astype(BF)
    d_router_w = dot_tn(normed_moe, lax.dynamic_slice_in_dim(logit_low, me * cols, cols, 1))

    spare = jnp.broadcast_to(summed_b[0, 0, 0, 0], (width, -cols % 128))
    d_mats = jnp.concatenate(
        [d_qkv_w.astype(BF), d_out_w.astype(BF), d_router_w.astype(BF), spare], axis=1
    )
    summed = lax.psum_scatter(
        row_major(d_mats), "row", scatter_dimension=0, tiled=True
    ).astype(F32)
    others = functools.reduce(lambda a, b: a + b.astype(F32), other_parts, zero_of(d_tokens))
    output = (hidden_state + own_part + others).astype(BF)

    gains = lax.psum(jnp.stack([d_attn_gain[0], d_query_gain, d_key_gain, d_moe_gain[0]]), "row")
    expert_grads = jnp.concatenate([summed_a, summed_b], axis=0)
    unpack = lambda i: jnp.transpose(expert_grads[:, i], (1, 0, 2)).astype(F32)
    cut = lambda i: summed[:, i * part : (i + 1) * part]
    return (
        output, d_tokens, gains[0], gains[1], gains[2], gains[3],
        cut(0), cut(1), cut(2), cut(3), summed[:, 4 * part : 4 * part + cols],
        unpack(0), unpack(1), unpack(2),
    )


def solution(mesh):
    grid = P("row", "col")
    cube = P("row", None, "col")
    rows = P("row", None)
    line = P("col")
    in_specs = (
        grid, line, line, line, line, grid, grid, grid, grid, grid,
        cube, cube, cube, rows, rows, grid,
    )
    out_specs = (
        grid, grid, line, line, line, line, grid, grid, grid, grid, grid, cube, cube, cube,
    )
    return jax.shard_map(shards, mesh=mesh, in_specs=in_specs, out_specs=out_specs, check_vma=False)
```

```python
import functools
import math

import jax
import jax.numpy as jnp
from jax import lax
from jax.experimental import pallas as pl
from jax.experimental.layout import Layout, with_layout_constraint
from jax.experimental.pallas import tpu as pltpu
from jax.sharding import PartitionSpec as P

HD = 128
IMG = 256

EPSILON = 1e-05
ROPE_BASE = 10000.0
MASKED = -1e30
VMEM_LIMIT = 66_000_000
BF = jnp.bfloat16
F32 = jnp.float32


def dot_nn(a, b):
    return lax.dot_general(a, b, (((1,), (0,)), ((), ())), preferred_element_type=F32)


def dot_nt(a, b):
    return lax.dot_general(a, b, (((1,), (1,)), ((), ())), preferred_element_type=F32)


def dot_tn(a, b):
    return lax.dot_general(a, b, (((0,), (0,)), ((), ())), preferred_element_type=F32)


def row_major(values):
    return with_layout_constraint(values, Layout(major_to_minor=tuple(range(values.ndim))))


def zero_of(values):
    return jnp.minimum(jnp.abs(values[(0,) * values.ndim].astype(F32)), 0.0).astype(BF)


def shift(values, k):
    n = lax.axis_size("col")
    return lax.ppermute(values, "col", [(i, (i + k) % n) for i in range(n)])


def pieces_line(block):
    n = lax.axis_size("col")
    far = {k: shift(block, k) for k in (*range(2, n), 1)}
    return [far[k] for k in range(1, n)]


def sum_small(values, more=0.0):
    n = lax.axis_size("col")
    total = values + more
    for k in range(1, n):
        total = total + lax.ppermute(values, "col", [(i, (i + k) % n) for i in range(n)])
    return total


def gather_small(values):
    n = lax.axis_size("col")
    me = lax.axis_index("col")
    out = jnp.zeros((n, *values.shape), values.dtype)
    out = lax.dynamic_update_index_in_dim(out, values, me, 0)
    for k in range(1, n):
        piece = lax.ppermute(values, "col", [(i, (i + k) % n) for i in range(n)])
        out = lax.dynamic_update_index_in_dim(out, piece, lax.rem(me - k + n, n), 0)
    return out


CHUNK = 128


def line_kernel(n, make, n_in, n_out, *refs):
    plan = make(refs[:n_in], refs[n_in : n_in + n_out])
    term, first, second, out = plan
    stat_out, stat_in, stat_sem, *rest = refs[n_in + n_out :]
    if term is not None:
        sums, held, sum_sem, *rest = rest
    if out is not None:
        (gather_sem,) = rest
    chunks = stat_out.shape[0]
    me = lax.axis_index("col")
    ways = ((1, me > 0, me < n - 1), (-1, me < n - 1, me > 0))

    barrier = pltpu.get_barrier_semaphore()
    for k in range(1, n):
        pl.semaphore_signal(
            barrier, inc=1, device_id={"col": lax.rem(me + k, n)},
            device_id_type=pl.DeviceIdType.MESH,
        )
    pl.semaphore_wait(barrier, n - 1)

    def at(c):
        return pl.ds(pl.multiple_of(c * CHUNK, CHUNK), CHUNK)

    def remote(ref, sems, index, other):
        return pltpu.make_async_remote_copy(
            src_ref=ref, dst_ref=ref, send_sem=sems.at[(0, *index)], recv_sem=sems.at[(1, *index)],
            device_id={"col": other}, device_id_type=pl.DeviceIdType.MESH,
        )

    def sum_copy(way, s, c, other):
        return remote(sums.at[way, s, at(c)], sum_sem, (way, s, c), other)

    def gather_copy(way, s, c, other):
        part = out.shape[1] // n
        block = out.at[at(c), pl.ds(pl.multiple_of(s * part, part), part)]
        return remote(block, gather_sem, (way, s, c), other)

    def stat_copy(k, c):
        return pltpu.make_async_remote_copy(
            src_ref=stat_out.at[c], dst_ref=stat_in.at[k, c], send_sem=stat_sem.at[0, k, c],
            recv_sem=stat_sem.at[1, k, c], device_id={"col": lax.rem(me + k, n)},
            device_id_type=pl.DeviceIdType.MESH,
        )

    def arrived(way, s, c):
        step, has_source, _ = ways[way]

        @pl.when(has_source)
        def _():
            sum_copy(way, s, c, me - step).wait_recv()

        @pl.when(jnp.logical_not(has_source))
        def _():
            sums[way, s, at(c)] = jnp.zeros_like(sums[way, s, at(c)])

    depths = (me, n - 1 - me)
    hops = []
    for j in range(n - 1):
        hops += [(0, n - 1 - j, n - 1 - j > me), (1, j, j < me)]

    def on_turn(t, hop, action):
        way, s, mine = hop
        c = t - depths[way]
        pl.when(mine & (c >= 0) & (c < chunks))(lambda: action(way, s, c))

    def ready(way, s, c):
        held[way] = term(at(c), s)

    def add(way, s, c):
        arrived(way, s, c)
        sums[way, s, at(c)] = (held[way] + sums[way, s, at(c)].astype(F32)).astype(BF)

    def send(way, s, c):
        sum_copy(way, s, c, me + ways[way][0]).start()

    def finish(c):
        total = None
        if term is not None:
            arrived(0, me, c)
            arrived(1, me, c)
            total = (
                term(at(c), me) + sums[0, me, at(c)].astype(F32) + sums[1, me, at(c)].astype(F32)
            )
        stat = jnp.broadcast_to(first(at(c), total), (CHUNK, 128))
        stat_out[c] = jnp.concatenate([stat] * (128 // CHUNK), axis=0).T[:8]

    def apply(c):
        row = stat_out[c]
        for k in range(1, n):
            stat_copy(k, c).wait_recv()
            row = row + stat_in[k, c]
        stat = jnp.broadcast_to(row[:1], (128, 128)).T[:CHUNK, :1]
        block = second(at(c), stat)
        if out is not None:
            part = out.shape[1] // n
            out[at(c), pl.ds(pl.multiple_of(me * part, part), part)] = block

    def pass_on(c, r):
        for way, (step, _, has_target) in enumerate(ways):
            s = me - step * r
            there = jnp.logical_and(s >= 0, s < n)
            if r > 0:
                @pl.when(there)
                def _():
                    gather_copy(way, s, c, me - step).wait_recv()

            @pl.when(jnp.logical_and(there, has_target))
            def _():
                gather_copy(way, s, c, me + step).start()

    lag = 0 if term is None else n - 1
    last = lag + 1 + (0 if out is None else n)

    def body(t, carry):
        def stage(delay, action):
            c = t - delay
            pl.when(jnp.logical_and(c >= 0, c < chunks))(lambda: action(c))

        if out is not None:
            for r in range(n - 1, -1, -1):
                stage(lag + 2 + r, lambda c: pass_on(c, r))
        if term is not None:
            on_turn(t, hops[0], ready)
            for hop, later in zip(hops, hops[1:]):
                on_turn(t, hop, add)
                on_turn(t, later, ready)
                on_turn(t, hop, send)
            on_turn(t, hops[-1], add)
        stage(lag, finish)
        if term is not None:
            on_turn(t, hops[-1], send)
        stage(lag + 1, apply)

        def tell(c):
            for k in range(1, n):
                stat_copy(k, c).start()

        stage(lag, tell)
        return carry

    lax.fori_loop(0, chunks + last + 1, body, 0)

    def drain(c, carry):
        for k in range(1, n):
            stat_copy(k, c).wait_send()
        if term is not None:
            for way, s, mine in hops:
                @pl.when(mine)
                def _():
                    sum_copy(way, s, c, me + ways[way][0]).wait_send()
        if out is not None:
            for r in range(n):
                for way, (step, _, has_target) in enumerate(ways):
                    s = me - step * r
                    there = jnp.logical_and(s >= 0, s < n)

                    @pl.when(jnp.logical_and(there, has_target))
                    def _():
                        gather_copy(way, s, c, me + step).wait_send()
        return carry

    lax.fori_loop(0, chunks, drain, 0)


def along_line(make, operands, out_shape, rows, part, sums, gathers, number, name):
    n = lax.axis_size("col")
    chunks = rows // CHUNK
    vmem = pl.BlockSpec(memory_space=pltpu.VMEM)
    scratch = [
        pltpu.VMEM((chunks, 8, 128), F32), pltpu.VMEM((n, chunks, 8, 128), F32),
        pltpu.SemaphoreType.DMA((2, n, chunks)),
    ]
    if sums:
        scratch += [
            pltpu.VMEM((2, n, rows, part), BF), pltpu.VMEM((2, CHUNK, part), F32),
            pltpu.SemaphoreType.DMA((2, 2, n, chunks)),
        ]
    if gathers:
        scratch += [pltpu.SemaphoreType.DMA((2, 2, n, chunks))]
    return pl.pallas_call(
        functools.partial(line_kernel, n, make, len(operands), len(out_shape)),
        in_specs=[vmem] * len(operands),
        out_specs=[vmem] * len(out_shape),
        out_shape=out_shape,
        scratch_shapes=scratch,
        compiler_params=pltpu.CompilerParams(
            vmem_limit_bytes=VMEM_LIMIT, collective_id=number, has_side_effects=True
        ),
        cost_estimate=pl.CostEstimate(
            flops=1_000_000, bytes_accessed=rows * part, transcendentals=0
        ),
        name=name,
    )(*operands)


def norm_line(tokens, gain, width):
    rows, part = tokens.shape

    def make(ins, outs):
        x_ref, gain_ref = ins
        out_ref, inv_ref = outs

        def first(at, total):
            x = x_ref[at, :].astype(F32)
            return jnp.sum(x * x, axis=1, keepdims=True)

        def second(at, stat):
            inv = lax.rsqrt(stat / width + EPSILON)
            inv_ref[at, :] = inv
            return (x_ref[at, :].astype(F32) * inv * gain_ref[...].astype(F32)).astype(BF)

        return None, first, second, out_ref

    out_shape = [
        jax.ShapeDtypeStruct((rows, width), BF), jax.ShapeDtypeStruct((rows, 1), F32)
    ]
    return along_line(make, [tokens, gain], out_shape, rows, part, False, True, 1, "norm_line")


def attn_line(mixed, w_out, tokens, gain, width):
    rows, part = tokens.shape

    def make(ins, outs):
        m_ref, w_ref, x_ref, gain_ref = ins
        out_ref, hidden_ref, inv_ref = outs

        def term(at, s):
            return dot_nt(m_ref[at, :], w_ref[pl.ds(s * part, part), :])

        def first(at, total):
            hidden = x_ref[at, :].astype(F32) + total
            hidden_ref[at, :] = hidden
            return jnp.sum(hidden * hidden, axis=1, keepdims=True)

        def second(at, stat):
            inv = lax.rsqrt(stat / width + EPSILON)
            inv_ref[at, :] = inv
            return (hidden_ref[at, :] * inv * gain_ref[...].astype(F32)).astype(BF)

        return term, first, second, out_ref

    out_shape = [
        jax.ShapeDtypeStruct((rows, width), BF), jax.ShapeDtypeStruct((rows, part), F32),
        jax.ShapeDtypeStruct((rows, 1), F32),
    ]
    return along_line(
        make, [mixed, w_out, tokens, gain], out_shape, rows, part, True, True, 2, "attn_line"
    )


def moe_line(terms, hidden, inv, gain, grads, width):
    rows, part = hidden.shape

    def make(ins, outs):
        t_ref, hidden_ref, inv_ref, gain_ref, y_ref = ins
        out_ref, grad_ref, d_gain_ref = outs
        d_gain_ref[...] = jnp.zeros_like(d_gain_ref)

        def term(at, s):
            return t_ref[s, at, :].astype(F32)

        def first(at, total):
            grad_ref[at, :] = total
            product = total * hidden_ref[at, :]
            d_gain_ref[...] += jnp.sum(product * inv_ref[at, :], axis=0, keepdims=True)
            return jnp.sum(product * gain_ref[...].astype(F32), axis=1, keepdims=True)

        def second(at, stat):
            factor = inv_ref[at, :]
            grad = (
                y_ref[at, :].astype(F32)
                + factor * gain_ref[...].astype(F32) * grad_ref[at, :]
                - factor * factor * factor * (stat / width) * hidden_ref[at, :]
            )
            grad_ref[at, :] = grad
            return grad.astype(BF)

        return term, first, second, out_ref

    out_shape = [
        jax.ShapeDtypeStruct((rows, width), BF), jax.ShapeDtypeStruct((rows, part), F32),
        jax.ShapeDtypeStruct((1, part), F32),
    ]
    return along_line(
        make, [terms, hidden, inv, gain, grads], out_shape, rows, part, True, True, 3, "moe_line"
    )


def input_line(qkv_grad, w_qkv, tokens, inv, gain, grads, width):
    rows, part = tokens.shape

    def make(ins, outs):
        q_ref, w_ref, x_ref, inv_ref, gain_ref, y_ref = ins
        grad_ref, d_gain_ref = outs
        d_gain_ref[...] = jnp.zeros_like(d_gain_ref)

        def term(at, s):
            return dot_nt(q_ref[at, :], w_ref[pl.ds(s * part, part), :])

        def first(at, total):
            grad_ref[at, :] = total
            product = total * x_ref[at, :].astype(F32)
            d_gain_ref[...] += jnp.sum(product * inv_ref[at, :], axis=0, keepdims=True)
            return jnp.sum(product * gain_ref[...].astype(F32), axis=1, keepdims=True)

        def second(at, stat):
            factor = inv_ref[at, :]
            grad_ref[at, :] = (
                y_ref[at, :]
                + factor * gain_ref[...].astype(F32) * grad_ref[at, :]
                - factor * factor * factor * (stat / width) * x_ref[at, :].astype(F32)
            )

        return term, first, second, None

    out_shape = [jax.ShapeDtypeStruct((rows, part), F32), jax.ShapeDtypeStruct((1, part), F32)]
    return along_line(
        make, [qkv_grad, w_qkv, tokens, inv, gain, grads], out_shape, rows, part, True, False, 4,
        "input_line",
    )


def rope_tables(length):
    half_size = HD // 2
    places = jnp.arange(length, dtype=F32)
    rates = jnp.exp(-math.log(ROPE_BASE) * jnp.arange(half_size, dtype=F32) / half_size)
    angles = places[:, None] * rates[None, :]
    cosine, sine = jnp.cos(angles), jnp.sin(angles)
    return jnp.concatenate([cosine, cosine], 1), jnp.concatenate([-sine, sine], 1)


def span_ids(starts, length):
    places = jnp.arange(length, dtype=jnp.int32)
    inside = (places[None, :] >= starts[:, None]) & (places[None, :] < starts[:, None] + IMG)
    numbers = jnp.arange(1, starts.shape[0] + 1, dtype=jnp.int32)
    return jnp.sum(jnp.where(inside, numbers[:, None], 0), axis=0)


def attend_kernel(
    scale, block, q_ref, k_ref, v_ref, iq_ref, ik_ref, gq_ref, gk_ref, cos_ref, sin_ref,
    srow_ref, scol_ref, qo_ref, ko_ref, vo_ref, mixed_ref
):
    rows = q_ref.shape[0]
    cosine, sine = cos_ref[...], sin_ref[...]

    def turned(raw_ref, inv_ref, gain_ref):
        normed = raw_ref[...] * inv_ref[...] * gain_ref[...].astype(F32)
        return (normed * cosine + pltpu.roll(normed, HD // 2, 1) * sine).astype(BF)

    qo_ref[...] = turned(q_ref, iq_ref, gq_ref)
    ko_ref[...] = turned(k_ref, ik_ref, gk_ref)
    vo_ref[...] = v_ref[...].astype(BF)
    for first in range(0, rows, block):
        last = min(rows, first + block + IMG)
        scores = dot_nt(qo_ref[first : first + block, :], ko_ref[:last, :]) * scale
        q_at = first + lax.broadcasted_iota(jnp.int32, scores.shape, 0)
        k_at = lax.broadcasted_iota(jnp.int32, scores.shape, 1)
        q_span = scol_ref[first : first + block, :]
        seen = (k_at <= q_at) | ((q_span == srow_ref[:, :last]) & (q_span > 0))
        scores = jnp.where(seen, scores, MASKED)
        raised = jnp.exp(scores - jnp.max(scores, axis=1, keepdims=True))
        probs = (raised / jnp.sum(raised, axis=1, keepdims=True)).astype(BF)
        mixed_ref[first : first + block, :] = dot_nn(probs, vo_ref[:last, :]).astype(BF)


def attend(qkv, inv_q, inv_k, gain_q, gain_k, cosine, sine, span_row, span_col):
    rows = qkv.shape[0]
    width = qkv.shape[1] // 3
    heads = width // HD
    head = lambda shift: pl.BlockSpec((rows, HD), lambda h: (0, h + shift * heads))
    whole = lambda shape: pl.BlockSpec(shape, lambda h: (0, 0))
    out = jax.ShapeDtypeStruct((rows, width), BF)
    return pl.pallas_call(
        functools.partial(attend_kernel, 1.0 / math.sqrt(HD), min(256, rows)),
        grid=(heads,),
        in_specs=[
            head(0), head(1), head(2), whole((rows, 1)), whole((rows, 1)),
            pl.BlockSpec((1, HD), lambda h: (0, h)), pl.BlockSpec((1, HD), lambda h: (0, h)),
            whole((rows, HD)), whole((rows, HD)), whole((1, rows)), whole((rows, 1)),
        ],
        out_specs=[head(0)] * 4,
        out_shape=[out] * 4,
        compiler_params=pltpu.CompilerParams(vmem_limit_bytes=VMEM_LIMIT),
        cost_estimate=pl.CostEstimate(
            flops=4 * rows * rows * width, bytes_accessed=20 * rows * width,
            transcendentals=rows * rows * heads,
        ),
        name="attend",
    )(qkv, qkv, qkv, inv_q, inv_k, gain_q, gain_k, cosine, sine, span_row, span_col)


def attend_back_kernel(
    scale, block, q_ref, k_ref, v_ref, d_ref, cos_ref, sin_ref, srow_ref, scol_ref, _,
    dq_ref, dk_ref, dv_ref, dk_sum, dv_sum
):
    rows = q_ref.shape[0]
    dk_sum[...] = jnp.zeros_like(dk_sum)
    dv_sum[...] = jnp.zeros_like(dv_sum)

    def turned(values, at):
        return values * cos_ref[at, :] - pltpu.roll(values, HD // 2, 1) * sin_ref[at, :]

    for first in range(0, rows, block):
        here = slice(first, first + block)
        last = min(rows, first + block + IMG)
        queries, keys, grads = q_ref[here, :], k_ref[:last, :], d_ref[here, :]
        scores = dot_nt(keys, queries) * scale
        k_at = lax.broadcasted_iota(jnp.int32, scores.shape, 0)
        q_at = first + lax.broadcasted_iota(jnp.int32, scores.shape, 1)
        q_span = srow_ref[:, here]
        seen = (k_at <= q_at) | ((q_span == scol_ref[:last, :]) & (q_span > 0))
        scores = jnp.where(seen, scores, MASKED)
        raised = jnp.exp(scores - jnp.max(scores, axis=0, keepdims=True))
        probs = raised / jnp.sum(raised, axis=0, keepdims=True)
        d_probs = dot_nt(v_ref[:last, :], grads)
        d_scores = (probs * (d_probs - jnp.sum(probs * d_probs, axis=0, keepdims=True))).astype(BF)
        dq_ref[here, :] = turned(dot_tn(d_scores, keys) * scale, here)
        dk_sum[:last, :] += dot_nn(d_scores, queries)
        dv_sum[:last, :] += dot_nn(probs.astype(BF), grads)
    dk_ref[...] = turned(dk_sum[...] * scale, slice(0, rows))
    dv_ref[...] = dv_sum[...].astype(BF)


def attend_back(queries, keys, values, grads, cosine, sine, span_row, span_col, earlier):
    rows, width = queries.shape
    heads = width // HD
    head = pl.BlockSpec((rows, HD), lambda h: (0, h))
    whole = lambda shape: pl.BlockSpec(shape, lambda h: (0, 0))
    return pl.pallas_call(
        functools.partial(attend_back_kernel, 1.0 / math.sqrt(HD), min(256, rows)),
        grid=(heads,),
        in_specs=[head] * 4
        + [whole((rows, HD)), whole((rows, HD)), whole((1, rows)), whole((rows, 1))]
        + [pl.BlockSpec(memory_space=pl.ANY)],
        out_specs=[head] * 3,
        out_shape=[
            jax.ShapeDtypeStruct((rows, width), F32),
            jax.ShapeDtypeStruct((rows, width), F32),
            jax.ShapeDtypeStruct((rows, width), BF),
        ],
        scratch_shapes=[pltpu.VMEM((rows, HD), F32)] * 2,
        compiler_params=pltpu.CompilerParams(vmem_limit_bytes=VMEM_LIMIT),
        cost_estimate=pl.CostEstimate(
            flops=10 * rows * rows * width, bytes_accessed=20 * rows * width,
            transcendentals=rows * rows * heads,
        ),
        name="attend_back",
    )(queries, keys, values, grads, cosine, sine, span_row, span_col, earlier)


def prepare_kernel(n, x_ref, own_ref, *refs):
    pieces, (_, xt_ref, y_ref, yt_ref) = refs[: n - 1], refs[n - 1 :]
    part = own_ref.shape[1]
    me = lax.axis_index("col")
    for s in range(n):
        cols = slice(s * part, (s + 1) * part)
        xt_ref[cols, :] = x_ref[:, cols].T
    for k, piece in enumerate((own_ref, *pieces)):
        cols = pl.ds(pl.multiple_of(lax.rem(me - k + n, n) * part, part), part)
        y_ref[:, cols] = piece[...]
        yt_ref[cols, :] = piece[...].T


def prepare(x, own, pieces, earlier):
    rows, width = x.shape
    part = own.shape[1]
    n = width // part
    step = min(256, rows)
    wide = pl.BlockSpec((step, width), lambda i: (i, 0))
    tall = pl.BlockSpec((width, step), lambda i: (0, i))
    block = pl.BlockSpec((step, part), lambda i: (i, 0))
    out = lambda a, b: jax.ShapeDtypeStruct((a, b), BF)
    return pl.pallas_call(
        functools.partial(prepare_kernel, n),
        grid=(rows // step,),
        in_specs=[wide] + [block] * n + [pl.BlockSpec(memory_space=pl.ANY)],
        out_specs=[tall, wide, tall],
        out_shape=[out(width, rows), out(rows, width), out(width, rows)],
        compiler_params=pltpu.CompilerParams(vmem_limit_bytes=VMEM_LIMIT),
        cost_estimate=pl.CostEstimate(
            flops=0, bytes_accessed=10 * rows * width, transcendentals=0
        ),
        name="prepare",
    )(x, own, *pieces, earlier)


def gate_of(gates_ref, at, span, expert):
    experts = gates_ref.shape[1]
    mine = lax.broadcasted_iota(jnp.int32, (span, experts), 1) == expert
    return mine, jnp.sum(jnp.where(mine, gates_ref[at, :], 0.0), axis=1, keepdims=True)


def forward_kernel(first, n_col, closing, x_ref, gates_ref, w_ref, *rest):
    if closing:
        first_ref, *rest = rest
    out_ref, pre_ref, up_ref, acc, hid = rest
    step = pl.program_id(0)
    rows, width = x_ref.shape
    units = w_ref.shape[-1]

    @pl.when(step == 0)
    def _():
        acc[...] = jnp.zeros_like(acc)

    w_gate = w_ref[:, 0, 0].reshape(width, units)
    w_up = w_ref[:, 0, 1].reshape(width, units)
    span = min(256, rows)
    for start in range(0, rows, span):
        at = slice(start, start + span)
        g, u = dot_nn(x_ref[at, :], w_gate), dot_nn(x_ref[at, :], w_up)
        _, gate = gate_of(gates_ref, at, span, step + first)
        hid[at, :] = (gate * (g / (1.0 + jnp.exp(-g)) * u)).astype(BF)
        pre_ref[0, at, :] = g.astype(BF)
        up_ref[0, at, :] = u.astype(BF)

    w_down = w_ref[:, 0, 2].reshape(width, units)
    part = width // n_col
    for s in range(n_col):
        cols = slice(s * part, (s + 1) * part)
        acc[:, cols] += dot_nt(hid[...], w_down[cols, :])

    @pl.when(step == pl.num_programs(0) - 1)
    def _():
        for s in range(n_col):
            total = acc[:, s * part : (s + 1) * part]
            if closing:
                total = total + first_ref[s].astype(F32)
            out_ref[s] = total.astype(BF)


def once(shape):
    return pl.BlockSpec(shape, lambda e: (0,) * len(shape), pipeline_mode=pl.Buffered(1))


def each(shape):
    return pl.BlockSpec((1, *shape), lambda e: (e,) + (0,) * len(shape))


def moe_forward(first, x, gates, weights, before):
    rows, width = x.shape
    n_row, here, _, depth, units = weights.shape
    n_col = lax.axis_size("col")
    block = pl.BlockSpec((n_row, 1, 3, depth, units), lambda e: (0, e, 0, 0, 0))
    blocks = (n_col, rows, width // n_col)
    more = [] if before is None else [before]
    hidden = jax.ShapeDtypeStruct((here, rows, units), BF)
    return pl.pallas_call(
        functools.partial(forward_kernel, first, n_col, before is not None),
        grid=(here,),
        in_specs=[once((rows, width)), once(gates.shape), block] + [once(a.shape) for a in more],
        out_specs=[once(blocks), each((rows, units)), each((rows, units))],
        out_shape=[jax.ShapeDtypeStruct(blocks, BF), hidden, hidden],
        scratch_shapes=[pltpu.VMEM((rows, width), F32)]
        + [pltpu.VMEM((rows, units), BF)],
        compiler_params=pltpu.CompilerParams(vmem_limit_bytes=VMEM_LIMIT),
        cost_estimate=pl.CostEstimate(
            flops=6 * here * rows * width * units,
            bytes_accessed=6 * here * n_row * depth * units + 8 * rows * width,
            transcendentals=here * rows * units,
        ),
        name="experts_forward",
    )(x, gates, weights, *more)


def backward_kernel(
    first, n_col, closing, xt_ref, y_ref, yt_ref, gates_ref, w_ref, pre_ref, up_ref, *rest
):
    if closing:
        probs_ref, before_ref, router_ref, first_ref, *rest = rest
        dx_ref, dw_ref, dg_ref, acc, hid, d_pre, d_up = rest
    else:
        parts_ref, dx_ref, dw_ref, dg_ref, got_ref, acc, hid, d_pre, d_up, sems = rest
    step = pl.program_id(0)
    rows, width = y_ref.shape
    me = lax.axis_index("col")

    def part_copy(k):
        other = lax.rem(me + k, n_col)
        return pltpu.make_async_remote_copy(
            src_ref=parts_ref.at[other], dst_ref=got_ref.at[k - 1], send_sem=sems.at[0, k - 1],
            recv_sem=sems.at[1, k - 1], device_id={"col": other},
            device_id_type=pl.DeviceIdType.MESH,
        )

    if not closing:
        @pl.when(step == 0)
        def _():
            barrier = pltpu.get_barrier_semaphore()
            for k in range(1, n_col):
                pl.semaphore_signal(
                    barrier, inc=1, device_id={"col": lax.rem(me + k, n_col)},
                    device_id_type=pl.DeviceIdType.MESH,
                )
            pl.semaphore_wait(barrier, n_col - 1)
            for k in range(1, n_col):
                part_copy(k).start()

        @pl.when(step == pl.num_programs(0) - 1)
        def _():
            for k in range(1, n_col):
                part_copy(k).wait()

    n_row, _, _, depth, units = w_ref.shape

    @pl.when(step == 0)
    def _():
        acc[...] = jnp.zeros_like(acc)
        dg_ref[...] = before_ref[...] if closing else jnp.zeros_like(dg_ref)

    w_gate = w_ref[:, 0, 0].reshape(width, units)
    w_up = w_ref[:, 0, 1].reshape(width, units)
    w_down = w_ref[:, 0, 2].reshape(width, units)
    span = min(256, rows)

    for start in range(0, rows, span):
        at = slice(start, start + span)
        dh = dot_nn(y_ref[at, :], w_down)
        g, u = pre_ref[0, at, :].astype(F32), up_ref[0, at, :].astype(F32)
        mine, gate = gate_of(gates_ref, at, span, step + first)
        s = 1.0 / (1.0 + jnp.exp(-g))
        silu = g * s
        both = silu * u
        hid[at, :] = (gate * both).astype(BF)
        d_gate = jnp.sum(dh * both, axis=1, keepdims=True)
        dg_ref[at, :] += jnp.where(mine, d_gate, 0.0)
        act = dh * gate
        d_pre[at, :] = (act * u * (s * (1.0 + g * (1.0 - s)))).astype(BF)
        d_up[at, :] = (act * silu).astype(BF)

    dw_ref[:, 0, 0] = dot_nn(xt_ref[...], d_pre[...]).astype(BF).reshape(n_row, depth, units)
    dw_ref[:, 0, 1] = dot_nn(xt_ref[...], d_up[...]).astype(BF).reshape(n_row, depth, units)
    dw_ref[:, 0, 2] = dot_nn(yt_ref[...], hid[...]).astype(BF).reshape(n_row, depth, units)
    part = width // n_col
    for s in range(n_col):
        cols = slice(s * part, (s + 1) * part)
        acc[:, cols] += dot_nt(d_pre[...], w_gate[cols, :]) + dot_nt(d_up[...], w_up[cols, :])

    @pl.when(step == pl.num_programs(0) - 1)
    def _():
        if closing:
            probs = probs_ref[...]
            g = jnp.where(gates_ref[...] > 0.0, dg_ref[...], 0.0)
            low = (probs * (g - jnp.sum(probs * g, axis=1, keepdims=True))).astype(BF)
        for s in range(n_col):
            cols = slice(s * part, (s + 1) * part)
            total = acc[:, cols]
            if closing:
                total = total + dot_nn(low, router_ref[:, cols]) + first_ref[s].astype(F32)
            dx_ref[s] = total.astype(BF)


def moe_backward(first, xt, y, yt, gates, weights, pre, up, parts, closing):
    rows, width = y.shape
    n_row, here, _, depth, units = weights.shape
    n_col = lax.axis_size("col")
    block = pl.BlockSpec((n_row, 1, 3, depth, units), lambda e: (0, e, 0, 0, 0))
    blocks = (n_col, rows, width // n_col)
    any_place = pl.BlockSpec(memory_space=pl.ANY)
    more = [parts] if closing is None else list(closing)
    more_specs = [any_place] if closing is None else [once(a.shape) for a in more]
    got, got_specs, sems, extra = [], [], [], {}
    if closing is None:
        got = [jax.ShapeDtypeStruct((n_col - 1, rows, width // n_col), BF)]
        got_specs = [any_place]
        sems = [pltpu.SemaphoreType.DMA((2, n_col - 1))]
        extra = {"collective_id": 5, "has_side_effects": True}
    return pl.pallas_call(
        functools.partial(backward_kernel, first, n_col, closing is not None),
        grid=(here,),
        in_specs=[
            once((width, rows)), once((rows, width)), once((width, rows)), once(gates.shape),
            block, each((rows, units)), each((rows, units)),
        ]
        + more_specs,
        out_specs=[once(blocks), block, once(gates.shape)] + got_specs,
        out_shape=[
            jax.ShapeDtypeStruct(blocks, BF), jax.ShapeDtypeStruct(weights.shape, BF),
            jax.ShapeDtypeStruct(gates.shape, F32),
        ]
        + got,
        scratch_shapes=[pltpu.VMEM((rows, width), F32)]
        + [pltpu.VMEM((rows, units), BF)] * 3
        + sems,
        compiler_params=pltpu.CompilerParams(vmem_limit_bytes=VMEM_LIMIT, **extra),
        cost_estimate=pl.CostEstimate(
            flops=12 * here * rows * width * units,
            bytes_accessed=12 * here * n_row * depth * units + 12 * rows * width,
            transcendentals=here * rows * units,
        ),
        name="experts_backward",
    )(xt, y, yt, gates, weights, pre, up, *more)


def pack_experts(w_gate, w_up, w_down, first, last):
    pick = lambda w: jnp.transpose(w[:, first:last], (1, 0, 2))
    return row_major(jnp.stack([pick(w_gate), pick(w_up), pick(w_down)], axis=1))


def shards(
    tokens, norm_attn, norm_query, norm_key, norm_moe, w_query, w_key, w_value, w_out, w_router,
    w_gate, w_up, w_down, routes, span_starts, cotangent,
):
    rows, part = tokens.shape
    n_col = lax.axis_size("col")
    me = lax.axis_index("col")
    width = part * n_col
    experts = w_gate.shape[1]
    half = experts // 2
    cols = w_router.shape[1]

    pad = (-(4 * part + cols)) % 128
    mats = jnp.concatenate(
        [w_query, w_key, w_value, w_out, w_router, jnp.zeros((w_router.shape[0], pad), BF)], axis=1
    )
    mats = lax.all_gather(mats, "row", axis=0, tiled=True)
    full_qkv = mats[:, : 3 * part]
    full_out = mats[:, 3 * part : 4 * part]
    first_half = lax.all_gather(pack_experts(w_gate, w_up, w_down, 0, half), "row", axis=0)
    second_half = lax.all_gather(pack_experts(w_gate, w_up, w_down, half, experts), "row", axis=0)

    attn_gain = norm_attn.reshape(1, part)
    normed_attn, inv_first = norm_line(tokens, attn_gain, width)
    qkv = dot_nn(normed_attn, full_qkv)
    query_raw, key_raw = qkv[:, :part], qkv[:, part : 2 * part]

    squares = sum_small(
        jnp.stack([jnp.sum(query_raw * query_raw, axis=1), jnp.sum(key_raw * key_raw, axis=1)])
    )
    inv_qk = lax.rsqrt(squares / width + EPSILON)
    query_inv, key_inv = inv_qk[0][:, None], inv_qk[1][:, None]
    query_gain, key_gain = norm_query.reshape(1, part), norm_key.reshape(1, part)
    cosine, sine = rope_tables(rows)
    span_of = span_ids(span_starts[0], rows)
    span_row, span_col = span_of[None, :], span_of[:, None]
    queries, keys, values, mixed = attend(
        qkv, query_inv, key_inv, query_gain, key_gain, cosine, sine, span_row, span_col
    )

    moe_gain = norm_moe.reshape(1, part)
    normed_moe, hidden_state, inv_second = attn_line(mixed, full_out, tokens, moe_gain, width)
    grad_pieces = pieces_line(cotangent + zero_of(normed_moe))

    router_t = gather_small(mats[:, 4 * part : 4 * part + cols].T).reshape(experts, width)
    router_probs = jax.nn.softmax(dot_nt(normed_moe, router_t), axis=1)
    expert_ids = jnp.arange(experts, dtype=jnp.int32)
    routed = jnp.any(routes[:, :, None] == expert_ids[None, None, :], axis=1)
    gate_table = jnp.where(routed, router_probs, 0.0)

    part_a, pre_a, up_a = moe_forward(0, normed_moe, gate_table, first_half, None)
    moe_parts, pre_b, up_b = moe_forward(half, normed_moe, gate_table, second_half, part_a)
    normed_moe_t, grad_full, grad_full_t = prepare(normed_moe, cotangent, grad_pieces, up_b)
    dx_a, dw_a, dg_a, other_parts = moe_backward(
        0, normed_moe_t, grad_full, grad_full_t, gate_table, first_half, pre_a, up_a, moe_parts,
        None,
    )
    own_part = lax.dynamic_index_in_dim(moe_parts, me, 0, keepdims=False).astype(F32)
    output = (hidden_state + own_part + jnp.sum(other_parts.astype(F32), axis=0)).astype(BF)
    dx_b, dw_b, dg_b = moe_backward(
        half, normed_moe_t, grad_full, grad_full_t, gate_table, second_half, pre_b, up_b,
        None, (router_probs, dg_a, router_t, dx_a),
    )
    summed_a = lax.psum_scatter(dw_a, "row", scatter_dimension=0)
    summed_b = lax.psum_scatter(dw_b, "row", scatter_dimension=0)
    attn_grad, hidden_grad, d_moe_gain = moe_line(
        dx_b, hidden_state, inv_second, moe_gain, cotangent, width
    )
    mixed_grad = dot_nn(attn_grad, full_out).astype(BF)
    d_out_w = dot_tn(attn_grad, mixed)

    query_turned, key_turned, value_grad = attend_back(
        queries, keys, values, mixed_grad, cosine, sine, span_row, span_col, summed_a
    )
    query_scaled = query_turned * query_gain.astype(F32)
    key_scaled = key_turned * key_gain.astype(F32)
    stats = sum_small(
        jnp.stack(
            [jnp.sum(query_scaled * query_raw, axis=1), jnp.sum(key_scaled * key_raw, axis=1)]
        )
    )
    d_query_gain = jnp.sum(query_turned * query_raw * query_inv, axis=0)
    d_key_gain = jnp.sum(key_turned * key_raw * key_inv, axis=0)
    query_raw_grad = (
        query_inv * query_scaled - query_inv**3 * query_raw * stats[0][:, None] / width
    ).astype(BF)
    key_raw_grad = (
        key_inv * key_scaled - key_inv**3 * key_raw * stats[1][:, None] / width
    ).astype(BF)
    qkv_grad = jnp.concatenate([query_raw_grad, key_raw_grad, value_grad], axis=1)
    d_tokens, d_attn_gain = input_line(
        qkv_grad, full_qkv, tokens, inv_first, attn_gain, hidden_grad, width
    )
    d_qkv_w = dot_tn(normed_attn, qkv_grad)

    gate_grad = jnp.where(routed, sum_small(dg_b.T, zero_of(attn_grad)).T, 0.0)
    logit_low = (
        router_probs * (gate_grad - jnp.sum(router_probs * gate_grad, axis=1, keepdims=True))
    ).astype(BF)
    d_router_w = dot_tn(normed_moe, lax.dynamic_slice_in_dim(logit_low, me * cols, cols, 1))

    spare = jnp.zeros((width, -cols % 128), BF)
    d_mats = jnp.concatenate(
        [d_qkv_w.astype(BF), d_out_w.astype(BF), d_router_w.astype(BF), spare], axis=1
    )
    summed = lax.psum_scatter(
        row_major(d_mats), "row", scatter_dimension=0, tiled=True
    ).astype(F32)
    gains = lax.psum(jnp.stack([d_attn_gain[0], d_query_gain, d_key_gain, d_moe_gain[0]]), "row")
    expert_grads = jnp.concatenate([summed_a, summed_b], axis=0) + zero_of(d_tokens)
    unpack = lambda i: jnp.transpose(expert_grads[:, i], (1, 0, 2)).astype(F32)
    cut = lambda i: summed[:, i * part : (i + 1) * part]
    return (
        output, d_tokens, gains[0], gains[1], gains[2], gains[3],
        cut(0), cut(1), cut(2), cut(3), summed[:, 4 * part : 4 * part + cols],
        unpack(0), unpack(1), unpack(2),
    )


def solution(mesh):
    grid = P("row", "col")
    cube = P("row", None, "col")
    rows = P("row", None)
    line = P("col")
    in_specs = (
        grid, line, line, line, line, grid, grid, grid, grid, grid,
        cube, cube, cube, rows, rows, grid,
    )
    out_specs = (
        grid, grid, line, line, line, line, grid, grid, grid, grid, grid, cube, cube, cube,
    )
    return jax.shard_map(shards, mesh=mesh, in_specs=in_specs, out_specs=out_specs, check_vma=False)
```

```python
import functools
import math

import jax
import jax.numpy as jnp
from jax import lax
from jax.experimental import pallas as pl
from jax.experimental.layout import Layout, with_layout_constraint
from jax.experimental.pallas import tpu as pltpu
from jax.sharding import PartitionSpec as P

HD = 128
IMG = 256

EPSILON = 1e-05
ROPE_BASE = 10000.0
MASKED = -1e30
VMEM_LIMIT = 66_000_000
BF = jnp.bfloat16
F32 = jnp.float32


def dot_nn(a, b):
    return lax.dot_general(a, b, (((1,), (0,)), ((), ())), preferred_element_type=F32)


def dot_nt(a, b):
    return lax.dot_general(a, b, (((1,), (1,)), ((), ())), preferred_element_type=F32)


def dot_tn(a, b):
    return lax.dot_general(a, b, (((0,), (0,)), ((), ())), preferred_element_type=F32)


def row_major(values):
    return with_layout_constraint(values, Layout(major_to_minor=tuple(range(values.ndim))))


def zero_of(values):
    return jnp.minimum(jnp.abs(values[(0,) * values.ndim].astype(F32)), 0.0).astype(BF)


def shift(values, k):
    n = lax.axis_size("col")
    return lax.ppermute(values, "col", [(i, (i + k) % n) for i in range(n)])


def pieces_line(block):
    n = lax.axis_size("col")
    far = {k: shift(block, k) for k in (*range(2, n), 1)}
    return [far[k] for k in range(1, n)]


def sum_small(values, more=0.0):
    n = lax.axis_size("col")
    total = values + more
    for k in range(1, n):
        total = total + lax.ppermute(values, "col", [(i, (i + k) % n) for i in range(n)])
    return total


def gather_small(values):
    n = lax.axis_size("col")
    me = lax.axis_index("col")
    out = jnp.zeros((n, *values.shape), values.dtype)
    out = lax.dynamic_update_index_in_dim(out, values, me, 0)
    for k in range(1, n):
        piece = lax.ppermute(values, "col", [(i, (i + k) % n) for i in range(n)])
        out = lax.dynamic_update_index_in_dim(out, piece, lax.rem(me - k + n, n), 0)
    return out


CHUNK = 128


def line_kernel(n, make, n_in, n_out, *refs):
    plan = make(refs[:n_in], refs[n_in : n_in + n_out])
    term, first, second, out = plan
    stat_out, stat_in, stat_sem, *rest = refs[n_in + n_out :]
    if term is not None:
        sums, held, sum_sem, *rest = rest
    if out is not None:
        (gather_sem,) = rest
    chunks = stat_out.shape[0]
    me = lax.axis_index("col")
    ways = ((1, me > 0, me < n - 1), (-1, me < n - 1, me > 0))

    barrier = pltpu.get_barrier_semaphore()
    for k in range(1, n):
        pl.semaphore_signal(
            barrier, inc=1, device_id={"col": lax.rem(me + k, n)},
            device_id_type=pl.DeviceIdType.MESH,
        )
    pl.semaphore_wait(barrier, n - 1)

    def at(c):
        return pl.ds(pl.multiple_of(c * CHUNK, CHUNK), CHUNK)

    def remote(ref, sems, index, other):
        return pltpu.make_async_remote_copy(
            src_ref=ref, dst_ref=ref, send_sem=sems.at[(0, *index)], recv_sem=sems.at[(1, *index)],
            device_id={"col": other}, device_id_type=pl.DeviceIdType.MESH,
        )

    def sum_copy(way, s, c, other):
        return remote(sums.at[way, s, at(c)], sum_sem, (way, s, c), other)

    def gather_copy(way, s, c, other):
        part = out.shape[1] // n
        block = out.at[at(c), pl.ds(pl.multiple_of(s * part, part), part)]
        return remote(block, gather_sem, (way, s, c), other)

    def stat_copy(k, c):
        return pltpu.make_async_remote_copy(
            src_ref=stat_out.at[c], dst_ref=stat_in.at[k, c], send_sem=stat_sem.at[0, k, c],
            recv_sem=stat_sem.at[1, k, c], device_id={"col": lax.rem(me + k, n)},
            device_id_type=pl.DeviceIdType.MESH,
        )

    def arrived(way, s, c):
        step, has_source, _ = ways[way]

        @pl.when(has_source)
        def _():
            sum_copy(way, s, c, me - step).wait_recv()

        @pl.when(jnp.logical_not(has_source))
        def _():
            sums[way, s, at(c)] = jnp.zeros_like(sums[way, s, at(c)])

    depths = (me, n - 1 - me)
    hops = []
    for j in range(n - 1):
        hops += [(0, n - 1 - j, n - 1 - j > me), (1, j, j < me)]

    def on_turn(t, hop, action):
        way, s, mine = hop
        c = t - depths[way]
        pl.when(mine & (c >= 0) & (c < chunks))(lambda: action(way, s, c))

    def ready(way, s, c):
        held[way] = term(at(c), s)

    def add(way, s, c):
        arrived(way, s, c)
        sums[way, s, at(c)] = (held[way] + sums[way, s, at(c)].astype(F32)).astype(BF)

    def send(way, s, c):
        sum_copy(way, s, c, me + ways[way][0]).start()

    def finish(c):
        total = None
        if term is not None:
            arrived(0, me, c)
            arrived(1, me, c)
            total = (
                term(at(c), me) + sums[0, me, at(c)].astype(F32) + sums[1, me, at(c)].astype(F32)
            )
        stat = jnp.broadcast_to(first(at(c), total), (CHUNK, 128))
        stat_out[c] = jnp.concatenate([stat] * (128 // CHUNK), axis=0).T[:8]

    def apply(c):
        row = stat_out[c]
        for k in range(1, n):
            stat_copy(k, c).wait_recv()
            row = row + stat_in[k, c]
        stat = jnp.broadcast_to(row[:1], (128, 128)).T[:CHUNK, :1]
        block = second(at(c), stat)
        if out is not None:
            part = out.shape[1] // n
            out[at(c), pl.ds(pl.multiple_of(me * part, part), part)] = block

    def pass_on(c, r):
        for way, (step, _, has_target) in enumerate(ways):
            s = me - step * r
            there = jnp.logical_and(s >= 0, s < n)
            if r > 0:
                @pl.when(there)
                def _():
                    gather_copy(way, s, c, me - step).wait_recv()

            @pl.when(jnp.logical_and(there, has_target))
            def _():
                gather_copy(way, s, c, me + step).start()

    lag = 0 if term is None else n - 1
    last = lag + (1 if out is None else n)

    def body(t, carry):
        def stage(delay, action):
            c = t - delay
            pl.when(jnp.logical_and(c >= 0, c < chunks))(lambda: action(c))

        if out is not None:
            for r in range(n - 1, 0, -1):
                stage(lag + 1 + r, lambda c: pass_on(c, r))
        if term is not None:
            on_turn(t, hops[0], ready)
            for hop, later in zip(hops, hops[1:]):
                on_turn(t, hop, add)
                on_turn(t, later, ready)
                on_turn(t, hop, send)
            on_turn(t, hops[-1], add)
        stage(lag + 1, apply)
        stage(lag, finish)
        if term is not None:
            on_turn(t, hops[-1], send)

        def tell(c):
            for k in range(1, n):
                stat_copy(k, c).start()

        stage(lag, tell)
        if out is not None:
            stage(lag + 1, lambda c: pass_on(c, 0))
        return carry

    lax.fori_loop(0, chunks + last, body, 0)

    def drain(c, carry):
        for k in range(1, n):
            stat_copy(k, c).wait_send()
        if term is not None:
            for way, s, mine in hops:
                @pl.when(mine)
                def _():
                    sum_copy(way, s, c, me + ways[way][0]).wait_send()
        if out is not None:
            for r in range(n):
                for way, (step, _, has_target) in enumerate(ways):
                    s = me - step * r
                    there = jnp.logical_and(s >= 0, s < n)

                    @pl.when(jnp.logical_and(there, has_target))
                    def _():
                        gather_copy(way, s, c, me + step).wait_send()
        return carry

    lax.fori_loop(0, chunks, drain, 0)


def along_line(make, operands, out_shape, rows, part, sums, gathers, number, name):
    n = lax.axis_size("col")
    chunks = rows // CHUNK
    vmem = pl.BlockSpec(memory_space=pltpu.VMEM)
    scratch = [
        pltpu.VMEM((chunks, 8, 128), F32), pltpu.VMEM((n, chunks, 8, 128), F32),
        pltpu.SemaphoreType.DMA((2, n, chunks)),
    ]
    if sums:
        scratch += [
            pltpu.VMEM((2, n, rows, part), BF), pltpu.VMEM((2, CHUNK, part), F32),
            pltpu.SemaphoreType.DMA((2, 2, n, chunks)),
        ]
    if gathers:
        scratch += [pltpu.SemaphoreType.DMA((2, 2, n, chunks))]
    return pl.pallas_call(
        functools.partial(line_kernel, n, make, len(operands), len(out_shape)),
        in_specs=[vmem] * len(operands),
        out_specs=[vmem] * len(out_shape),
        out_shape=out_shape,
        scratch_shapes=scratch,
        compiler_params=pltpu.CompilerParams(
            vmem_limit_bytes=VMEM_LIMIT, collective_id=number, has_side_effects=True
        ),
        cost_estimate=pl.CostEstimate(
            flops=1_000_000, bytes_accessed=rows * part, transcendentals=0
        ),
        name=name,
    )(*operands)


def norm_line(tokens, gain, width):
    rows, part = tokens.shape

    def make(ins, outs):
        x_ref, gain_ref = ins
        out_ref, inv_ref = outs

        def first(at, total):
            x = x_ref[at, :].astype(F32)
            return jnp.sum(x * x, axis=1, keepdims=True)

        def second(at, stat):
            inv = lax.rsqrt(stat / width + EPSILON)
            inv_ref[at, :] = inv
            return (x_ref[at, :].astype(F32) * inv * gain_ref[...].astype(F32)).astype(BF)

        return None, first, second, out_ref

    out_shape = [
        jax.ShapeDtypeStruct((rows, width), BF), jax.ShapeDtypeStruct((rows, 1), F32)
    ]
    return along_line(make, [tokens, gain], out_shape, rows, part, False, True, 1, "norm_line")


def attn_line(mixed, w_out, tokens, gain, width):
    rows, part = tokens.shape

    def make(ins, outs):
        m_ref, w_ref, x_ref, gain_ref = ins
        out_ref, hidden_ref, inv_ref = outs

        def term(at, s):
            return dot_nt(m_ref[at, :], w_ref[pl.ds(s * part, part), :])

        def first(at, total):
            hidden = x_ref[at, :].astype(F32) + total
            hidden_ref[at, :] = hidden
            return jnp.sum(hidden * hidden, axis=1, keepdims=True)

        def second(at, stat):
            inv = lax.rsqrt(stat / width + EPSILON)
            inv_ref[at, :] = inv
            return (hidden_ref[at, :] * inv * gain_ref[...].astype(F32)).astype(BF)

        return term, first, second, out_ref

    out_shape = [
        jax.ShapeDtypeStruct((rows, width), BF), jax.ShapeDtypeStruct((rows, part), F32),
        jax.ShapeDtypeStruct((rows, 1), F32),
    ]
    return along_line(
        make, [mixed, w_out, tokens, gain], out_shape, rows, part, True, True, 2, "attn_line"
    )


def moe_line(terms, hidden, inv, gain, grads, width):
    rows, part = hidden.shape

    def make(ins, outs):
        t_ref, hidden_ref, inv_ref, gain_ref, y_ref = ins
        out_ref, grad_ref, d_gain_ref = outs
        d_gain_ref[...] = jnp.zeros_like(d_gain_ref)

        def term(at, s):
            return t_ref[s, at, :].astype(F32)

        def first(at, total):
            grad_ref[at, :] = total
            product = total * hidden_ref[at, :]
            d_gain_ref[...] += jnp.sum(product * inv_ref[at, :], axis=0, keepdims=True)
            return jnp.sum(product * gain_ref[...].astype(F32), axis=1, keepdims=True)

        def second(at, stat):
            factor = inv_ref[at, :]
            grad = (
                y_ref[at, :].astype(F32)
                + factor * gain_ref[...].astype(F32) * grad_ref[at, :]
                - factor * factor * factor * (stat / width) * hidden_ref[at, :]
            )
            grad_ref[at, :] = grad
            return grad.astype(BF)

        return term, first, second, out_ref

    out_shape = [
        jax.ShapeDtypeStruct((rows, width), BF), jax.ShapeDtypeStruct((rows, part), F32),
        jax.ShapeDtypeStruct((1, part), F32),
    ]
    return along_line(
        make, [terms, hidden, inv, gain, grads], out_shape, rows, part, True, True, 3, "moe_line"
    )


def input_line(qkv_grad, w_qkv, tokens, inv, gain, grads, width):
    rows, part = tokens.shape

    def make(ins, outs):
        q_ref, w_ref, x_ref, inv_ref, gain_ref, y_ref = ins
        grad_ref, d_gain_ref = outs
        d_gain_ref[...] = jnp.zeros_like(d_gain_ref)

        def term(at, s):
            return dot_nt(q_ref[at, :], w_ref[pl.ds(s * part, part), :])

        def first(at, total):
            grad_ref[at, :] = total
            product = total * x_ref[at, :].astype(F32)
            d_gain_ref[...] += jnp.sum(product * inv_ref[at, :], axis=0, keepdims=True)
            return jnp.sum(product * gain_ref[...].astype(F32), axis=1, keepdims=True)

        def second(at, stat):
            factor = inv_ref[at, :]
            grad_ref[at, :] = (
                y_ref[at, :]
                + factor * gain_ref[...].astype(F32) * grad_ref[at, :]
                - factor * factor * factor * (stat / width) * x_ref[at, :].astype(F32)
            )

        return term, first, second, None

    out_shape = [jax.ShapeDtypeStruct((rows, part), F32), jax.ShapeDtypeStruct((1, part), F32)]
    return along_line(
        make, [qkv_grad, w_qkv, tokens, inv, gain, grads], out_shape, rows, part, True, False, 4,
        "input_line",
    )


def rope_tables(length):
    half_size = HD // 2
    places = jnp.arange(length, dtype=F32)
    rates = jnp.exp(-math.log(ROPE_BASE) * jnp.arange(half_size, dtype=F32) / half_size)
    angles = places[:, None] * rates[None, :]
    cosine, sine = jnp.cos(angles), jnp.sin(angles)
    return jnp.concatenate([cosine, cosine], 1), jnp.concatenate([-sine, sine], 1)


def span_ids(starts, length):
    places = jnp.arange(length, dtype=jnp.int32)
    inside = (places[None, :] >= starts[:, None]) & (places[None, :] < starts[:, None] + IMG)
    numbers = jnp.arange(1, starts.shape[0] + 1, dtype=jnp.int32)
    return jnp.sum(jnp.where(inside, numbers[:, None], 0), axis=0)


def attend_kernel(
    scale, block, q_ref, k_ref, v_ref, iq_ref, ik_ref, gq_ref, gk_ref, cos_ref, sin_ref,
    srow_ref, scol_ref, qo_ref, ko_ref, vo_ref, mixed_ref
):
    rows = q_ref.shape[0]
    cosine, sine = cos_ref[...], sin_ref[...]

    def turned(raw_ref, inv_ref, gain_ref):
        normed = raw_ref[...] * inv_ref[...] * gain_ref[...].astype(F32)
        return (normed * cosine + pltpu.roll(normed, HD // 2, 1) * sine).astype(BF)

    qo_ref[...] = turned(q_ref, iq_ref, gq_ref)
    ko_ref[...] = turned(k_ref, ik_ref, gk_ref)
    vo_ref[...] = v_ref[...].astype(BF)
    for first in range(0, rows, block):
        last = min(rows, first + block + IMG)
        scores = dot_nt(qo_ref[first : first + block, :], ko_ref[:last, :]) * scale
        q_at = first + lax.broadcasted_iota(jnp.int32, scores.shape, 0)
        k_at = lax.broadcasted_iota(jnp.int32, scores.shape, 1)
        q_span = scol_ref[first : first + block, :]
        seen = (k_at <= q_at) | ((q_span == srow_ref[:, :last]) & (q_span > 0))
        scores = jnp.where(seen, scores, MASKED)
        raised = jnp.exp(scores - jnp.max(scores, axis=1, keepdims=True))
        probs = (raised / jnp.sum(raised, axis=1, keepdims=True)).astype(BF)
        mixed_ref[first : first + block, :] = dot_nn(probs, vo_ref[:last, :]).astype(BF)


def attend(qkv, inv_q, inv_k, gain_q, gain_k, cosine, sine, span_row, span_col):
    rows = qkv.shape[0]
    width = qkv.shape[1] // 3
    heads = width // HD
    head = lambda shift: pl.BlockSpec((rows, HD), lambda h: (0, h + shift * heads))
    whole = lambda shape: pl.BlockSpec(shape, lambda h: (0, 0))
    out = jax.ShapeDtypeStruct((rows, width), BF)
    return pl.pallas_call(
        functools.partial(attend_kernel, 1.0 / math.sqrt(HD), min(256, rows)),
        grid=(heads,),
        in_specs=[
            head(0), head(1), head(2), whole((rows, 1)), whole((rows, 1)),
            pl.BlockSpec((1, HD), lambda h: (0, h)), pl.BlockSpec((1, HD), lambda h: (0, h)),
            whole((rows, HD)), whole((rows, HD)), whole((1, rows)), whole((rows, 1)),
        ],
        out_specs=[head(0)] * 4,
        out_shape=[out] * 4,
        compiler_params=pltpu.CompilerParams(vmem_limit_bytes=VMEM_LIMIT),
        cost_estimate=pl.CostEstimate(
            flops=4 * rows * rows * width, bytes_accessed=20 * rows * width,
            transcendentals=rows * rows * heads,
        ),
        name="attend",
    )(qkv, qkv, qkv, inv_q, inv_k, gain_q, gain_k, cosine, sine, span_row, span_col)


def attend_back_kernel(
    scale, block, q_ref, k_ref, v_ref, d_ref, cos_ref, sin_ref, srow_ref, scol_ref, _,
    dq_ref, dk_ref, dv_ref, dk_sum, dv_sum
):
    rows = q_ref.shape[0]
    dk_sum[...] = jnp.zeros_like(dk_sum)
    dv_sum[...] = jnp.zeros_like(dv_sum)

    def turned(values, at):
        return values * cos_ref[at, :] - pltpu.roll(values, HD // 2, 1) * sin_ref[at, :]

    for first in range(0, rows, block):
        here = slice(first, first + block)
        last = min(rows, first + block + IMG)
        queries, keys, grads = q_ref[here, :], k_ref[:last, :], d_ref[here, :]
        scores = dot_nt(keys, queries) * scale
        k_at = lax.broadcasted_iota(jnp.int32, scores.shape, 0)
        q_at = first + lax.broadcasted_iota(jnp.int32, scores.shape, 1)
        q_span = srow_ref[:, here]
        seen = (k_at <= q_at) | ((q_span == scol_ref[:last, :]) & (q_span > 0))
        scores = jnp.where(seen, scores, MASKED)
        raised = jnp.exp(scores - jnp.max(scores, axis=0, keepdims=True))
        probs = raised / jnp.sum(raised, axis=0, keepdims=True)
        d_probs = dot_nt(v_ref[:last, :], grads)
        d_scores = (probs * (d_probs - jnp.sum(probs * d_probs, axis=0, keepdims=True))).astype(BF)
        dq_ref[here, :] = turned(dot_tn(d_scores, keys) * scale, here)
        dk_sum[:last, :] += dot_nn(d_scores, queries)
        dv_sum[:last, :] += dot_nn(probs.astype(BF), grads)
    dk_ref[...] = turned(dk_sum[...] * scale, slice(0, rows))
    dv_ref[...] = dv_sum[...].astype(BF)


def attend_back(queries, keys, values, grads, cosine, sine, span_row, span_col, earlier):
    rows, width = queries.shape
    heads = width // HD
    head = pl.BlockSpec((rows, HD), lambda h: (0, h))
    whole = lambda shape: pl.BlockSpec(shape, lambda h: (0, 0))
    return pl.pallas_call(
        functools.partial(attend_back_kernel, 1.0 / math.sqrt(HD), min(256, rows)),
        grid=(heads,),
        in_specs=[head] * 4
        + [whole((rows, HD)), whole((rows, HD)), whole((1, rows)), whole((rows, 1))]
        + [pl.BlockSpec(memory_space=pl.ANY)],
        out_specs=[head] * 3,
        out_shape=[
            jax.ShapeDtypeStruct((rows, width), F32),
            jax.ShapeDtypeStruct((rows, width), F32),
            jax.ShapeDtypeStruct((rows, width), BF),
        ],
        scratch_shapes=[pltpu.VMEM((rows, HD), F32)] * 2,
        compiler_params=pltpu.CompilerParams(vmem_limit_bytes=VMEM_LIMIT),
        cost_estimate=pl.CostEstimate(
            flops=10 * rows * rows * width, bytes_accessed=20 * rows * width,
            transcendentals=rows * rows * heads,
        ),
        name="attend_back",
    )(queries, keys, values, grads, cosine, sine, span_row, span_col, earlier)


def prepare_kernel(n, x_ref, own_ref, *refs):
    pieces, (_, xt_ref, y_ref, yt_ref) = refs[: n - 1], refs[n - 1 :]
    part = own_ref.shape[1]
    me = lax.axis_index("col")
    for s in range(n):
        cols = slice(s * part, (s + 1) * part)
        xt_ref[cols, :] = x_ref[:, cols].T
    for k, piece in enumerate((own_ref, *pieces)):
        cols = pl.ds(pl.multiple_of(lax.rem(me - k + n, n) * part, part), part)
        y_ref[:, cols] = piece[...]
        yt_ref[cols, :] = piece[...].T


def prepare(x, own, pieces, earlier):
    rows, width = x.shape
    part = own.shape[1]
    n = width // part
    step = min(256, rows)
    wide = pl.BlockSpec((step, width), lambda i: (i, 0))
    tall = pl.BlockSpec((width, step), lambda i: (0, i))
    block = pl.BlockSpec((step, part), lambda i: (i, 0))
    out = lambda a, b: jax.ShapeDtypeStruct((a, b), BF)
    return pl.pallas_call(
        functools.partial(prepare_kernel, n),
        grid=(rows // step,),
        in_specs=[wide] + [block] * n + [pl.BlockSpec(memory_space=pl.ANY)],
        out_specs=[tall, wide, tall],
        out_shape=[out(width, rows), out(rows, width), out(width, rows)],
        compiler_params=pltpu.CompilerParams(vmem_limit_bytes=VMEM_LIMIT),
        cost_estimate=pl.CostEstimate(
            flops=0, bytes_accessed=10 * rows * width, transcendentals=0
        ),
        name="prepare",
    )(x, own, *pieces, earlier)


def gate_of(gates_ref, at, span, expert):
    experts = gates_ref.shape[1]
    mine = lax.broadcasted_iota(jnp.int32, (span, experts), 1) == expert
    return mine, jnp.sum(jnp.where(mine, gates_ref[at, :], 0.0), axis=1, keepdims=True)


def forward_kernel(first, n_col, closing, x_ref, gates_ref, w_ref, *rest):
    if closing:
        first_ref, *rest = rest
    out_ref, pre_ref, up_ref, acc, hid = rest
    step = pl.program_id(0)
    rows, width = x_ref.shape
    units = w_ref.shape[-1]

    @pl.when(step == 0)
    def _():
        acc[...] = jnp.zeros_like(acc)

    w_gate = w_ref[:, 0, 0].reshape(width, units)
    w_up = w_ref[:, 0, 1].reshape(width, units)
    span = min(256, rows)
    for start in range(0, rows, span):
        at = slice(start, start + span)
        g, u = dot_nn(x_ref[at, :], w_gate), dot_nn(x_ref[at, :], w_up)
        _, gate = gate_of(gates_ref, at, span, step + first)
        hid[at, :] = (gate * (g / (1.0 + jnp.exp(-g)) * u)).astype(BF)
        pre_ref[0, at, :] = g.astype(BF)
        up_ref[0, at, :] = u.astype(BF)

    w_down = w_ref[:, 0, 2].reshape(width, units)
    part = width // n_col
    for s in range(n_col):
        cols = slice(s * part, (s + 1) * part)
        acc[:, cols] += dot_nt(hid[...], w_down[cols, :])

    @pl.when(step == pl.num_programs(0) - 1)
    def _():
        for s in range(n_col):
            total = acc[:, s * part : (s + 1) * part]
            if closing:
                total = total + first_ref[s].astype(F32)
            out_ref[s] = total.astype(BF)


def once(shape):
    return pl.BlockSpec(shape, lambda e: (0,) * len(shape), pipeline_mode=pl.Buffered(1))


def each(shape):
    return pl.BlockSpec((1, *shape), lambda e: (e,) + (0,) * len(shape))


def moe_forward(first, x, gates, weights, before):
    rows, width = x.shape
    n_row, here, _, depth, units = weights.shape
    n_col = lax.axis_size("col")
    block = pl.BlockSpec((n_row, 1, 3, depth, units), lambda e: (0, e, 0, 0, 0))
    blocks = (n_col, rows, width // n_col)
    more = [] if before is None else [before]
    hidden = jax.ShapeDtypeStruct((here, rows, units), BF)
    return pl.pallas_call(
        functools.partial(forward_kernel, first, n_col, before is not None),
        grid=(here,),
        in_specs=[once((rows, width)), once(gates.shape), block] + [once(a.shape) for a in more],
        out_specs=[once(blocks), each((rows, units)), each((rows, units))],
        out_shape=[jax.ShapeDtypeStruct(blocks, BF), hidden, hidden],
        scratch_shapes=[pltpu.VMEM((rows, width), F32)]
        + [pltpu.VMEM((rows, units), BF)],
        compiler_params=pltpu.CompilerParams(vmem_limit_bytes=VMEM_LIMIT),
        cost_estimate=pl.CostEstimate(
            flops=6 * here * rows * width * units,
            bytes_accessed=6 * here * n_row * depth * units + 8 * rows * width,
            transcendentals=here * rows * units,
        ),
        name="experts_forward",
    )(x, gates, weights, *more)


def backward_kernel(
    first, n_col, closing, xt_ref, y_ref, yt_ref, gates_ref, w_ref, pre_ref, up_ref, *rest
):
    if closing:
        probs_ref, before_ref, router_ref, first_ref, *rest = rest
    parts_ref, dx_ref, dw_ref, dg_ref, got_ref, acc, hid, d_pre, d_up, sems = rest
    step = pl.program_id(0)
    rows, width = y_ref.shape
    me = lax.axis_index("col")

    def part_copy(k):
        other = lax.rem(me + k, n_col)
        count = rows // 2
        return pltpu.make_async_remote_copy(
            src_ref=parts_ref.at[other, pl.ds(count if closing else 0, count)], dst_ref=got_ref.at[k - 1], send_sem=sems.at[0, k - 1],
            recv_sem=sems.at[1, k - 1], device_id={"col": other},
            device_id_type=pl.DeviceIdType.MESH,
        )

    @pl.when(step == 0)
    def _():
        barrier = pltpu.get_barrier_semaphore()
        for k in range(1, n_col):
            pl.semaphore_signal(
                barrier, inc=1, device_id={"col": lax.rem(me + k, n_col)},
                device_id_type=pl.DeviceIdType.MESH,
            )
        pl.semaphore_wait(barrier, n_col - 1)
        for k in range(1, n_col):
            part_copy(k).start()

    @pl.when(step == pl.num_programs(0) - 1)
    def _():
        for k in range(1, n_col):
            part_copy(k).wait()

    n_row, _, _, depth, units = w_ref.shape

    @pl.when(step == 0)
    def _():
        acc[...] = jnp.zeros_like(acc)
        dg_ref[...] = before_ref[...] if closing else jnp.zeros_like(dg_ref)

    w_gate = w_ref[:, 0, 0].reshape(width, units)
    w_up = w_ref[:, 0, 1].reshape(width, units)
    w_down = w_ref[:, 0, 2].reshape(width, units)
    span = min(256, rows)

    for start in range(0, rows, span):
        at = slice(start, start + span)
        dh = dot_nn(y_ref[at, :], w_down)
        g, u = pre_ref[0, at, :].astype(F32), up_ref[0, at, :].astype(F32)
        mine, gate = gate_of(gates_ref, at, span, step + first)
        s = 1.0 / (1.0 + jnp.exp(-g))
        silu = g * s
        both = silu * u
        hid[at, :] = (gate * both).astype(BF)
        d_gate = jnp.sum(dh * both, axis=1, keepdims=True)
        dg_ref[at, :] += jnp.where(mine, d_gate, 0.0)
        act = dh * gate
        d_pre[at, :] = (act * u * (s * (1.0 + g * (1.0 - s)))).astype(BF)
        d_up[at, :] = (act * silu).astype(BF)

    dw_ref[:, 0, 0] = dot_nn(xt_ref[...], d_pre[...]).astype(BF).reshape(n_row, depth, units)
    dw_ref[:, 0, 1] = dot_nn(xt_ref[...], d_up[...]).astype(BF).reshape(n_row, depth, units)
    dw_ref[:, 0, 2] = dot_nn(yt_ref[...], hid[...]).astype(BF).reshape(n_row, depth, units)
    part = width // n_col
    for s in range(n_col):
        cols = slice(s * part, (s + 1) * part)
        acc[:, cols] += dot_nt(d_pre[...], w_gate[cols, :]) + dot_nt(d_up[...], w_up[cols, :])

    @pl.when(step == pl.num_programs(0) - 1)
    def _():
        if closing:
            probs = probs_ref[...]
            g = jnp.where(gates_ref[...] > 0.0, dg_ref[...], 0.0)
            low = (probs * (g - jnp.sum(probs * g, axis=1, keepdims=True))).astype(BF)
        for s in range(n_col):
            cols = slice(s * part, (s + 1) * part)
            total = acc[:, cols]
            if closing:
                total = total + dot_nn(low, router_ref[:, cols]) + first_ref[s].astype(F32)
            dx_ref[s] = total.astype(BF)


def moe_backward(first, xt, y, yt, gates, weights, pre, up, parts, closing):
    rows, width = y.shape
    n_row, here, _, depth, units = weights.shape
    n_col = lax.axis_size("col")
    block = pl.BlockSpec((n_row, 1, 3, depth, units), lambda e: (0, e, 0, 0, 0))
    blocks = (n_col, rows, width // n_col)
    any_place = pl.BlockSpec(memory_space=pl.ANY)
    more = list(closing or ())
    more_specs = [once(a.shape) for a in more] + [any_place]
    more.append(parts)
    got = [jax.ShapeDtypeStruct((n_col - 1, rows // 2, width // n_col), BF)]
    sems = [pltpu.SemaphoreType.DMA((2, n_col - 1))]
    extra = {"collective_id": 5 if closing is None else 6, "has_side_effects": True}
    return pl.pallas_call(
        functools.partial(backward_kernel, first, n_col, closing is not None),
        grid=(here,),
        in_specs=[
            once((width, rows)), once((rows, width)), once((width, rows)), once(gates.shape),
            block, each((rows, units)), each((rows, units)),
        ]
        + more_specs,
        out_specs=[once(blocks), block, once(gates.shape), any_place],
        out_shape=[
            jax.ShapeDtypeStruct(blocks, BF), jax.ShapeDtypeStruct(weights.shape, BF),
            jax.ShapeDtypeStruct(gates.shape, F32),
        ]
        + got,
        scratch_shapes=[pltpu.VMEM((rows, width), F32)]
        + [pltpu.VMEM((rows, units), BF)] * 3
        + sems,
        compiler_params=pltpu.CompilerParams(vmem_limit_bytes=VMEM_LIMIT, **extra),
        cost_estimate=pl.CostEstimate(
            flops=12 * here * rows * width * units,
            bytes_accessed=12 * here * n_row * depth * units + 12 * rows * width,
            transcendentals=here * rows * units,
        ),
        name="experts_backward",
    )(xt, y, yt, gates, weights, pre, up, *more)


def pack_experts(w_gate, w_up, w_down, first, last):
    pick = lambda w: jnp.transpose(w[:, first:last], (1, 0, 2))
    return row_major(jnp.stack([pick(w_gate), pick(w_up), pick(w_down)], axis=1))


def shards(
    tokens, norm_attn, norm_query, norm_key, norm_moe, w_query, w_key, w_value, w_out, w_router,
    w_gate, w_up, w_down, routes, span_starts, cotangent,
):
    rows, part = tokens.shape
    n_col = lax.axis_size("col")
    me = lax.axis_index("col")
    width = part * n_col
    experts = w_gate.shape[1]
    half = experts // 2
    cols = w_router.shape[1]

    pad = (-(4 * part + cols)) % 128
    mats = jnp.concatenate(
        [w_query, w_key, w_value, w_out, w_router, jnp.zeros((w_router.shape[0], pad), BF)], axis=1
    )
    mats = lax.all_gather(mats, "row", axis=0, tiled=True)
    full_qkv = mats[:, : 3 * part]
    full_out = mats[:, 3 * part : 4 * part]
    first_half = lax.all_gather(pack_experts(w_gate, w_up, w_down, 0, half), "row", axis=0)
    second_half = lax.all_gather(pack_experts(w_gate, w_up, w_down, half, experts), "row", axis=0)

    attn_gain = norm_attn.reshape(1, part)
    normed_attn, inv_first = norm_line(tokens, attn_gain, width)
    qkv = dot_nn(normed_attn, full_qkv)
    query_raw, key_raw = qkv[:, :part], qkv[:, part : 2 * part]

    squares = sum_small(
        jnp.stack([jnp.sum(query_raw * query_raw, axis=1), jnp.sum(key_raw * key_raw, axis=1)])
    )
    inv_qk = lax.rsqrt(squares / width + EPSILON)
    query_inv, key_inv = inv_qk[0][:, None], inv_qk[1][:, None]
    query_gain, key_gain = norm_query.reshape(1, part), norm_key.reshape(1, part)
    cosine, sine = rope_tables(rows)
    span_of = span_ids(span_starts[0], rows)
    span_row, span_col = span_of[None, :], span_of[:, None]
    queries, keys, values, mixed = attend(
        qkv, query_inv, key_inv, query_gain, key_gain, cosine, sine, span_row, span_col
    )

    moe_gain = norm_moe.reshape(1, part)
    normed_moe, hidden_state, inv_second = attn_line(mixed, full_out, tokens, moe_gain, width)
    grad_pieces = pieces_line(cotangent + zero_of(normed_moe))

    router_t = gather_small(mats[:, 4 * part : 4 * part + cols].T).reshape(experts, width)
    router_probs = jax.nn.softmax(dot_nt(normed_moe, router_t), axis=1)
    expert_ids = jnp.arange(experts, dtype=jnp.int32)
    routed = jnp.any(routes[:, :, None] == expert_ids[None, None, :], axis=1)
    gate_table = jnp.where(routed, router_probs, 0.0)

    part_a, pre_a, up_a = moe_forward(0, normed_moe, gate_table, first_half, None)
    moe_parts, pre_b, up_b = moe_forward(half, normed_moe, gate_table, second_half, part_a)
    normed_moe_t, grad_full, grad_full_t = prepare(normed_moe, cotangent, grad_pieces, up_b)
    dx_a, dw_a, dg_a, parts_a = moe_backward(
        0, normed_moe_t, grad_full, grad_full_t, gate_table, first_half, pre_a, up_a, moe_parts,
        None,
    )
    dx_b, dw_b, dg_b, parts_b = moe_backward(
        half, normed_moe_t, grad_full, grad_full_t, gate_table, second_half, pre_b, up_b,
        moe_parts, (router_probs, dg_a, router_t, dx_a),
    )
    summed_a = lax.psum_scatter(dw_a, "row", scatter_dimension=0)
    summed_b = lax.psum_scatter(dw_b, "row", scatter_dimension=0)
    attn_grad, hidden_grad, d_moe_gain = moe_line(
        dx_b, hidden_state, inv_second, moe_gain, cotangent, width
    )
    mixed_grad = dot_nn(attn_grad, full_out).astype(BF)
    d_out_w = dot_tn(attn_grad, mixed)

    query_turned, key_turned, value_grad = attend_back(
        queries, keys, values, mixed_grad, cosine, sine, span_row, span_col, summed_a
    )
    query_scaled = query_turned * query_gain.astype(F32)
    key_scaled = key_turned * key_gain.astype(F32)
    stats = sum_small(
        jnp.stack(
            [jnp.sum(query_scaled * query_raw, axis=1), jnp.sum(key_scaled * key_raw, axis=1)]
        )
    )
    d_query_gain = jnp.sum(query_turned * query_raw * query_inv, axis=0)
    d_key_gain = jnp.sum(key_turned * key_raw * key_inv, axis=0)
    query_raw_grad = (
        query_inv * query_scaled - query_inv**3 * query_raw * stats[0][:, None] / width
    ).astype(BF)
    key_raw_grad = (
        key_inv * key_scaled - key_inv**3 * key_raw * stats[1][:, None] / width
    ).astype(BF)
    qkv_grad = jnp.concatenate([query_raw_grad, key_raw_grad, value_grad], axis=1)
    d_tokens, d_attn_gain = input_line(
        qkv_grad, full_qkv, tokens, inv_first, attn_gain, hidden_grad, width
    )
    d_qkv_w = dot_tn(normed_attn, qkv_grad)

    gate_grad = jnp.where(routed, sum_small(dg_b.T + zero_of(attn_grad), zero_of(query_turned)).T, 0.0)
    logit_low = (
        router_probs * (gate_grad - jnp.sum(router_probs * gate_grad, axis=1, keepdims=True))
    ).astype(BF)
    d_router_w = dot_tn(normed_moe, lax.dynamic_slice_in_dim(logit_low, me * cols, cols, 1))

    spare = jnp.zeros((width, -cols % 128), BF)
    d_mats = jnp.concatenate(
        [d_qkv_w.astype(BF), d_out_w.astype(BF), d_router_w.astype(BF), spare], axis=1
    )
    summed = lax.psum_scatter(
        row_major(d_mats), "row", scatter_dimension=0, tiled=True
    ).astype(F32)
    own_part = lax.dynamic_index_in_dim(moe_parts, me, 0, keepdims=False).astype(F32)
    other_parts = jnp.concatenate([parts_a, parts_b], axis=1) + zero_of(d_tokens)
    output = (hidden_state + own_part + jnp.sum(other_parts.astype(F32), axis=0)).astype(BF)

    gains = lax.psum(jnp.stack([d_attn_gain[0], d_query_gain, d_key_gain, d_moe_gain[0]]), "row")
    expert_grads = jnp.concatenate([summed_a, summed_b], axis=0) + zero_of(d_tokens)
    unpack = lambda i: jnp.transpose(expert_grads[:, i], (1, 0, 2)).astype(F32)
    cut = lambda i: summed[:, i * part : (i + 1) * part]
    return (
        output, d_tokens, gains[0], gains[1], gains[2], gains[3],
        cut(0), cut(1), cut(2), cut(3), summed[:, 4 * part : 4 * part + cols],
        unpack(0), unpack(1), unpack(2),
    )


def solution(mesh):
    grid = P("row", "col")
    cube = P("row", None, "col")
    rows = P("row", None)
    line = P("col")
    in_specs = (
        grid, line, line, line, line, grid, grid, grid, grid, grid,
        cube, cube, cube, rows, rows, grid,
    )
    out_specs = (
        grid, grid, line, line, line, line, grid, grid, grid, grid, grid, cube, cube, cube,
    )
    return jax.shard_map(shards, mesh=mesh, in_specs=in_specs, out_specs=out_specs, check_vma=False)
```

```python
import functools
import math

import jax
import jax.numpy as jnp
from jax import lax
from jax.experimental import pallas as pl
from jax.experimental.layout import Layout, with_layout_constraint
from jax.experimental.pallas import tpu as pltpu
from jax.sharding import PartitionSpec as P

HD = 128
IMG = 256

EPSILON = 1e-05
ROPE_BASE = 10000.0
MASKED = -1e30
VMEM_LIMIT = 66_000_000
BF = jnp.bfloat16
F32 = jnp.float32


def dot_nn(a, b):
    return lax.dot_general(a, b, (((1,), (0,)), ((), ())), preferred_element_type=F32)


def dot_nt(a, b):
    return lax.dot_general(a, b, (((1,), (1,)), ((), ())), preferred_element_type=F32)


def dot_tn(a, b):
    return lax.dot_general(a, b, (((0,), (0,)), ((), ())), preferred_element_type=F32)


def row_major(values):
    return with_layout_constraint(values, Layout(major_to_minor=tuple(range(values.ndim))))


def zero_of(values):
    return jnp.minimum(jnp.abs(values[(0,) * values.ndim].astype(F32)), 0.0).astype(BF)


def shift(values, k):
    n = lax.axis_size("col")
    return lax.ppermute(values, "col", [(i, (i + k) % n) for i in range(n)])


def pieces_line(block):
    n = lax.axis_size("col")
    far = {k: shift(block, k) for k in (*range(2, n), 1)}
    return [far[k] for k in range(1, n)]


def sum_small(values, more=0.0):
    n = lax.axis_size("col")
    total = values + more
    for k in range(1, n):
        total = total + lax.ppermute(values, "col", [(i, (i + k) % n) for i in range(n)])
    return total


def gather_small(values):
    n = lax.axis_size("col")
    me = lax.axis_index("col")
    out = jnp.zeros((n, *values.shape), values.dtype)
    out = lax.dynamic_update_index_in_dim(out, values, me, 0)
    for k in range(1, n):
        piece = lax.ppermute(values, "col", [(i, (i + k) % n) for i in range(n)])
        out = lax.dynamic_update_index_in_dim(out, piece, lax.rem(me - k + n, n), 0)
    return out


CHUNK = 128


def line_kernel(n, make, n_in, n_out, *refs):
    plan = make(refs[:n_in], refs[n_in : n_in + n_out])
    term, first, second, out = plan
    stat_out, stat_in, stat_sem, *rest = refs[n_in + n_out :]
    if term is not None:
        sums, held, sum_sem, *rest = rest
    if out is not None:
        (gather_sem,) = rest
    chunks = stat_out.shape[0]
    me = lax.axis_index("col")
    ways = ((1, me > 0, me < n - 1), (-1, me < n - 1, me > 0))

    barrier = pltpu.get_barrier_semaphore()
    for k in range(1, n):
        pl.semaphore_signal(
            barrier, inc=1, device_id={"col": lax.rem(me + k, n)},
            device_id_type=pl.DeviceIdType.MESH,
        )
    pl.semaphore_wait(barrier, n - 1)

    def at(c):
        return pl.ds(pl.multiple_of(c * CHUNK, CHUNK), CHUNK)

    def remote(ref, sems, index, other):
        return pltpu.make_async_remote_copy(
            src_ref=ref, dst_ref=ref, send_sem=sems.at[(0, *index)], recv_sem=sems.at[(1, *index)],
            device_id={"col": other}, device_id_type=pl.DeviceIdType.MESH,
        )

    def sum_copy(way, s, c, other):
        return remote(sums.at[way, s, at(c)], sum_sem, (way, s, c), other)

    def gather_copy(way, s, c, other):
        part = out.shape[1] // n
        block = out.at[at(c), pl.ds(pl.multiple_of(s * part, part), part)]
        return remote(block, gather_sem, (way, s, c), other)

    def stat_copy(k, c):
        return pltpu.make_async_remote_copy(
            src_ref=stat_out.at[c], dst_ref=stat_in.at[k, c], send_sem=stat_sem.at[0, k, c],
            recv_sem=stat_sem.at[1, k, c], device_id={"col": lax.rem(me + k, n)},
            device_id_type=pl.DeviceIdType.MESH,
        )

    def arrived(way, s, c):
        step, has_source, _ = ways[way]

        @pl.when(has_source)
        def _():
            sum_copy(way, s, c, me - step).wait_recv()

        @pl.when(jnp.logical_not(has_source))
        def _():
            sums[way, s, at(c)] = jnp.zeros_like(sums[way, s, at(c)])

    depths = (me, n - 1 - me)
    hops = []
    for j in range(n - 1):
        hops += [(0, n - 1 - j, n - 1 - j > me), (1, j, j < me)]

    def on_turn(t, hop, action):
        way, s, mine = hop
        c = t - depths[way]
        pl.when(mine & (c >= 0) & (c < chunks))(lambda: action(way, s, c))

    def ready(way, s, c):
        held[way] = term(at(c), s)

    def add(way, s, c):
        arrived(way, s, c)
        sums[way, s, at(c)] = (held[way] + sums[way, s, at(c)].astype(F32)).astype(BF)

    def send(way, s, c):
        sum_copy(way, s, c, me + ways[way][0]).start()

    def finish(c):
        total = None
        if term is not None:
            arrived(0, me, c)
            arrived(1, me, c)
            total = (
                term(at(c), me) + sums[0, me, at(c)].astype(F32) + sums[1, me, at(c)].astype(F32)
            )
        stat = jnp.broadcast_to(first(at(c), total), (CHUNK, 128))
        stat_out[c] = jnp.concatenate([stat] * (128 // CHUNK), axis=0).T[:8]

    def apply(c):
        row = stat_out[c]
        for k in range(1, n):
            stat_copy(k, c).wait_recv()
            row = row + stat_in[k, c]
        stat = jnp.broadcast_to(row[:1], (128, 128)).T[:CHUNK, :1]
        block = second(at(c), stat)
        if out is not None:
            part = out.shape[1] // n
            out[at(c), pl.ds(pl.multiple_of(me * part, part), part)] = block

    def pass_on(c, r):
        for way, (step, _, has_target) in enumerate(ways):
            s = me - step * r
            there = jnp.logical_and(s >= 0, s < n)
            if r > 0:
                @pl.when(there)
                def _():
                    gather_copy(way, s, c, me - step).wait_recv()

            @pl.when(jnp.logical_and(there, has_target))
            def _():
                gather_copy(way, s, c, me + step).start()

    lag = 0 if term is None else n - 1
    last = lag + (1 if out is None else n)

    def body(t, carry):
        def stage(delay, action):
            c = t - delay
            pl.when(jnp.logical_and(c >= 0, c < chunks))(lambda: action(c))

        if out is not None:
            for r in range(n - 1, 0, -1):
                stage(lag + 1 + r, lambda c: pass_on(c, r))
        if term is not None:
            on_turn(t, hops[0], ready)
            for hop, later in zip(hops, hops[1:]):
                on_turn(t, hop, add)
                on_turn(t, later, ready)
                on_turn(t, hop, send)
            on_turn(t, hops[-1], add)
        stage(lag + 1, apply)
        stage(lag, finish)
        if term is not None:
            on_turn(t, hops[-1], send)

        def tell(c):
            for k in range(1, n):
                stat_copy(k, c).start()

        stage(lag, tell)
        if out is not None:
            stage(lag + 1, lambda c: pass_on(c, 0))
        return carry

    lax.fori_loop(0, chunks + last, body, 0)

    def drain(c, carry):
        for k in range(1, n):
            stat_copy(k, c).wait_send()
        if term is not None:
            for way, s, mine in hops:
                @pl.when(mine)
                def _():
                    sum_copy(way, s, c, me + ways[way][0]).wait_send()
        if out is not None:
            for r in range(n):
                for way, (step, _, has_target) in enumerate(ways):
                    s = me - step * r
                    there = jnp.logical_and(s >= 0, s < n)

                    @pl.when(jnp.logical_and(there, has_target))
                    def _():
                        gather_copy(way, s, c, me + step).wait_send()
        return carry

    lax.fori_loop(0, chunks, drain, 0)


def along_line(make, operands, out_shape, rows, part, sums, gathers, number, name):
    n = lax.axis_size("col")
    chunks = rows // CHUNK
    vmem = pl.BlockSpec(memory_space=pltpu.VMEM)
    scratch = [
        pltpu.VMEM((chunks, 8, 128), F32), pltpu.VMEM((n, chunks, 8, 128), F32),
        pltpu.SemaphoreType.DMA((2, n, chunks)),
    ]
    if sums:
        scratch += [
            pltpu.VMEM((2, n, rows, part), BF), pltpu.VMEM((2, CHUNK, part), F32),
            pltpu.SemaphoreType.DMA((2, 2, n, chunks)),
        ]
    if gathers:
        scratch += [pltpu.SemaphoreType.DMA((2, 2, n, chunks))]
    return pl.pallas_call(
        functools.partial(line_kernel, n, make, len(operands), len(out_shape)),
        in_specs=[vmem] * len(operands),
        out_specs=[vmem] * len(out_shape),
        out_shape=out_shape,
        scratch_shapes=scratch,
        compiler_params=pltpu.CompilerParams(
            vmem_limit_bytes=VMEM_LIMIT, collective_id=number, has_side_effects=True
        ),
        cost_estimate=pl.CostEstimate(
            flops=1_000_000, bytes_accessed=rows * part, transcendentals=0
        ),
        name=name,
    )(*operands)


def norm_line(tokens, gain, width):
    rows, part = tokens.shape

    def make(ins, outs):
        x_ref, gain_ref = ins
        out_ref, inv_ref = outs

        def first(at, total):
            x = x_ref[at, :].astype(F32)
            return jnp.sum(x * x, axis=1, keepdims=True)

        def second(at, stat):
            inv = lax.rsqrt(stat / width + EPSILON)
            inv_ref[at, :] = inv
            return (x_ref[at, :].astype(F32) * inv * gain_ref[...].astype(F32)).astype(BF)

        return None, first, second, out_ref

    out_shape = [
        jax.ShapeDtypeStruct((rows, width), BF), jax.ShapeDtypeStruct((rows, 1), F32)
    ]
    return along_line(make, [tokens, gain], out_shape, rows, part, False, True, 1, "norm_line")


def attn_line(mixed, w_out, tokens, gain, width):
    rows, part = tokens.shape

    def make(ins, outs):
        m_ref, w_ref, x_ref, gain_ref = ins
        out_ref, hidden_ref, inv_ref = outs

        def term(at, s):
            return dot_nt(m_ref[at, :], w_ref[pl.ds(s * part, part), :])

        def first(at, total):
            hidden = x_ref[at, :].astype(F32) + total
            hidden_ref[at, :] = hidden
            return jnp.sum(hidden * hidden, axis=1, keepdims=True)

        def second(at, stat):
            inv = lax.rsqrt(stat / width + EPSILON)
            inv_ref[at, :] = inv
            return (hidden_ref[at, :] * inv * gain_ref[...].astype(F32)).astype(BF)

        return term, first, second, out_ref

    out_shape = [
        jax.ShapeDtypeStruct((rows, width), BF), jax.ShapeDtypeStruct((rows, part), F32),
        jax.ShapeDtypeStruct((rows, 1), F32),
    ]
    return along_line(
        make, [mixed, w_out, tokens, gain], out_shape, rows, part, True, True, 2, "attn_line"
    )


def moe_line(terms, hidden, inv, gain, grads, width):
    rows, part = hidden.shape

    def make(ins, outs):
        t_ref, hidden_ref, inv_ref, gain_ref, y_ref = ins
        out_ref, grad_ref, d_gain_ref = outs
        d_gain_ref[...] = jnp.zeros_like(d_gain_ref)

        def term(at, s):
            return t_ref[s, at, :].astype(F32)

        def first(at, total):
            grad_ref[at, :] = total
            product = total * hidden_ref[at, :]
            d_gain_ref[...] += jnp.sum(product * inv_ref[at, :], axis=0, keepdims=True)
            return jnp.sum(product * gain_ref[...].astype(F32), axis=1, keepdims=True)

        def second(at, stat):
            factor = inv_ref[at, :]
            grad = (
                y_ref[at, :].astype(F32)
                + factor * gain_ref[...].astype(F32) * grad_ref[at, :]
                - factor * factor * factor * (stat / width) * hidden_ref[at, :]
            )
            grad_ref[at, :] = grad
            return grad.astype(BF)

        return term, first, second, out_ref

    out_shape = [
        jax.ShapeDtypeStruct((rows, width), BF), jax.ShapeDtypeStruct((rows, part), F32),
        jax.ShapeDtypeStruct((1, part), F32),
    ]
    return along_line(
        make, [terms, hidden, inv, gain, grads], out_shape, rows, part, True, True, 3, "moe_line"
    )


def input_line(qkv_grad, w_qkv, tokens, inv, gain, grads, width):
    rows, part = tokens.shape

    def make(ins, outs):
        q_ref, w_ref, x_ref, inv_ref, gain_ref, y_ref = ins
        grad_ref, d_gain_ref = outs
        d_gain_ref[...] = jnp.zeros_like(d_gain_ref)

        def term(at, s):
            return dot_nt(q_ref[at, :], w_ref[pl.ds(s * part, part), : q_ref.shape[1]])

        def first(at, total):
            grad_ref[at, :] = total
            product = total * x_ref[at, :].astype(F32)
            d_gain_ref[...] += jnp.sum(product * inv_ref[at, :], axis=0, keepdims=True)
            return jnp.sum(product * gain_ref[...].astype(F32), axis=1, keepdims=True)

        def second(at, stat):
            factor = inv_ref[at, :]
            grad_ref[at, :] = (
                y_ref[at, :]
                + factor * gain_ref[...].astype(F32) * grad_ref[at, :]
                - factor * factor * factor * (stat / width) * x_ref[at, :].astype(F32)
            )

        return term, first, second, None

    out_shape = [jax.ShapeDtypeStruct((rows, part), F32), jax.ShapeDtypeStruct((1, part), F32)]
    return along_line(
        make, [qkv_grad, w_qkv, tokens, inv, gain, grads], out_shape, rows, part, True, False, 4,
        "input_line",
    )


def rope_tables(length):
    half_size = HD // 2
    places = jnp.arange(length, dtype=F32)
    rates = jnp.exp(-math.log(ROPE_BASE) * jnp.arange(half_size, dtype=F32) / half_size)
    angles = places[:, None] * rates[None, :]
    cosine, sine = jnp.cos(angles), jnp.sin(angles)
    return jnp.concatenate([cosine, cosine], 1), jnp.concatenate([-sine, sine], 1)


def span_ids(starts, length):
    places = jnp.arange(length, dtype=jnp.int32)
    inside = (places[None, :] >= starts[:, None]) & (places[None, :] < starts[:, None] + IMG)
    numbers = jnp.arange(1, starts.shape[0] + 1, dtype=jnp.int32)
    return jnp.sum(jnp.where(inside, numbers[:, None], 0), axis=0)


def attend_kernel(
    scale, block, q_ref, k_ref, v_ref, iq_ref, ik_ref, gq_ref, gk_ref, cos_ref, sin_ref,
    srow_ref, scol_ref, qo_ref, ko_ref, vo_ref, mixed_ref
):
    rows = q_ref.shape[0]
    cosine, sine = cos_ref[...], sin_ref[...]

    def turned(raw_ref, inv_ref, gain_ref):
        normed = raw_ref[...] * inv_ref[...] * gain_ref[...].astype(F32)
        return (normed * cosine + pltpu.roll(normed, HD // 2, 1) * sine).astype(BF)

    qo_ref[...] = turned(q_ref, iq_ref, gq_ref)
    ko_ref[...] = turned(k_ref, ik_ref, gk_ref)
    vo_ref[...] = v_ref[...].astype(BF)
    for first in range(0, rows, block):
        last = min(rows, first + block + IMG)
        scores = dot_nt(qo_ref[first : first + block, :], ko_ref[:last, :]) * scale
        q_at = first + lax.broadcasted_iota(jnp.int32, scores.shape, 0)
        k_at = lax.broadcasted_iota(jnp.int32, scores.shape, 1)
        q_span = scol_ref[first : first + block, :]
        seen = (k_at <= q_at) | ((q_span == srow_ref[:, :last]) & (q_span > 0))
        scores = jnp.where(seen, scores, MASKED)
        raised = jnp.exp(scores - jnp.max(scores, axis=1, keepdims=True))
        probs = (raised / jnp.sum(raised, axis=1, keepdims=True)).astype(BF)
        mixed_ref[first : first + block, :] = dot_nn(probs, vo_ref[:last, :]).astype(BF)


def attend(qkv, inv_q, inv_k, gain_q, gain_k, cosine, sine, span_row, span_col):
    rows = qkv.shape[0]
    width = qkv.shape[1] // 3
    heads = width // HD
    head = lambda shift: pl.BlockSpec((rows, HD), lambda h: (0, h + shift * heads))
    whole = lambda shape: pl.BlockSpec(shape, lambda h: (0, 0))
    out = jax.ShapeDtypeStruct((rows, width), BF)
    return pl.pallas_call(
        functools.partial(attend_kernel, 1.0 / math.sqrt(HD), min(256, rows)),
        grid=(heads,),
        in_specs=[
            head(0), head(1), head(2), whole((rows, 1)), whole((rows, 1)),
            pl.BlockSpec((1, HD), lambda h: (0, h)), pl.BlockSpec((1, HD), lambda h: (0, h)),
            whole((rows, HD)), whole((rows, HD)), whole((1, rows)), whole((rows, 1)),
        ],
        out_specs=[head(0)] * 4,
        out_shape=[out] * 4,
        compiler_params=pltpu.CompilerParams(vmem_limit_bytes=VMEM_LIMIT),
        cost_estimate=pl.CostEstimate(
            flops=4 * rows * rows * width, bytes_accessed=20 * rows * width,
            transcendentals=rows * rows * heads,
        ),
        name="attend",
    )(qkv, qkv, qkv, inv_q, inv_k, gain_q, gain_k, cosine, sine, span_row, span_col)


def attend_back_kernel(
    scale, block, q_ref, k_ref, v_ref, d_ref, cos_ref, sin_ref, srow_ref, scol_ref, _,
    dq_ref, dk_ref, dv_ref, dk_sum, dv_sum
):
    rows = q_ref.shape[0]
    dk_sum[...] = jnp.zeros_like(dk_sum)
    dv_sum[...] = jnp.zeros_like(dv_sum)

    def turned(values, at):
        return values * cos_ref[at, :] - pltpu.roll(values, HD // 2, 1) * sin_ref[at, :]

    for first in range(0, rows, block):
        here = slice(first, first + block)
        last = min(rows, first + block + IMG)
        queries, keys, grads = q_ref[here, :], k_ref[:last, :], d_ref[here, :]
        scores = dot_nt(keys, queries) * scale
        k_at = lax.broadcasted_iota(jnp.int32, scores.shape, 0)
        q_at = first + lax.broadcasted_iota(jnp.int32, scores.shape, 1)
        q_span = srow_ref[:, here]
        seen = (k_at <= q_at) | ((q_span == scol_ref[:last, :]) & (q_span > 0))
        scores = jnp.where(seen, scores, MASKED)
        raised = jnp.exp(scores - jnp.max(scores, axis=0, keepdims=True))
        probs = raised / jnp.sum(raised, axis=0, keepdims=True)
        d_probs = dot_nt(v_ref[:last, :], grads)
        d_scores = (probs * (d_probs - jnp.sum(probs * d_probs, axis=0, keepdims=True))).astype(BF)
        dq_ref[here, :] = turned(dot_tn(d_scores, keys) * scale, here)
        dk_sum[:last, :] += dot_nn(d_scores, queries)
        dv_sum[:last, :] += dot_nn(probs.astype(BF), grads)
    dk_ref[...] = turned(dk_sum[...] * scale, slice(0, rows))
    dv_ref[...] = dv_sum[...].astype(BF)


def attend_back(queries, keys, values, grads, cosine, sine, span_row, span_col, earlier):
    rows, width = queries.shape
    heads = width // HD
    head = pl.BlockSpec((rows, HD), lambda h: (0, h))
    whole = lambda shape: pl.BlockSpec(shape, lambda h: (0, 0))
    return pl.pallas_call(
        functools.partial(attend_back_kernel, 1.0 / math.sqrt(HD), min(256, rows)),
        grid=(heads,),
        in_specs=[head] * 4
        + [whole((rows, HD)), whole((rows, HD)), whole((1, rows)), whole((rows, 1))]
        + [pl.BlockSpec(memory_space=pl.ANY)],
        out_specs=[head] * 3,
        out_shape=[
            jax.ShapeDtypeStruct((rows, width), F32),
            jax.ShapeDtypeStruct((rows, width), F32),
            jax.ShapeDtypeStruct((rows, width), BF),
        ],
        scratch_shapes=[pltpu.VMEM((rows, HD), F32)] * 2,
        compiler_params=pltpu.CompilerParams(vmem_limit_bytes=VMEM_LIMIT),
        cost_estimate=pl.CostEstimate(
            flops=10 * rows * rows * width, bytes_accessed=20 * rows * width,
            transcendentals=rows * rows * heads,
        ),
        name="attend_back",
    )(queries, keys, values, grads, cosine, sine, span_row, span_col, earlier)


def prepare_kernel(n, x_ref, own_ref, *refs):
    pieces, (_, xt_ref, y_ref, yt_ref) = refs[: n - 1], refs[n - 1 :]
    part = own_ref.shape[1]
    me = lax.axis_index("col")
    for s in range(n):
        cols = slice(s * part, (s + 1) * part)
        xt_ref[cols, :] = x_ref[:, cols].T
    for k, piece in enumerate((own_ref, *pieces)):
        cols = pl.ds(pl.multiple_of(lax.rem(me - k + n, n) * part, part), part)
        y_ref[:, cols] = piece[...]
        yt_ref[cols, :] = piece[...].T


def prepare(x, own, pieces, earlier):
    rows, width = x.shape
    part = own.shape[1]
    n = width // part
    step = min(256, rows)
    wide = pl.BlockSpec((step, width), lambda i: (i, 0))
    tall = pl.BlockSpec((width, step), lambda i: (0, i))
    block = pl.BlockSpec((step, part), lambda i: (i, 0))
    out = lambda a, b: jax.ShapeDtypeStruct((a, b), BF)
    return pl.pallas_call(
        functools.partial(prepare_kernel, n),
        grid=(rows // step,),
        in_specs=[wide] + [block] * n + [pl.BlockSpec(memory_space=pl.ANY)],
        out_specs=[tall, wide, tall],
        out_shape=[out(width, rows), out(rows, width), out(width, rows)],
        compiler_params=pltpu.CompilerParams(vmem_limit_bytes=VMEM_LIMIT),
        cost_estimate=pl.CostEstimate(
            flops=0, bytes_accessed=10 * rows * width, transcendentals=0
        ),
        name="prepare",
    )(x, own, *pieces, earlier)


def gate_of(gates_ref, at, span, expert):
    experts = gates_ref.shape[1]
    mine = lax.broadcasted_iota(jnp.int32, (span, experts), 1) == expert
    return mine, jnp.sum(jnp.where(mine, gates_ref[at, :], 0.0), axis=1, keepdims=True)


def forward_kernel(first, n_col, closing, x_ref, gates_ref, w_ref, *rest):
    if closing:
        first_ref, *rest = rest
    out_ref, pre_ref, up_ref, acc, hid = rest
    step = pl.program_id(0)
    rows, width = x_ref.shape
    units = w_ref.shape[-1]

    @pl.when(step == 0)
    def _():
        acc[...] = jnp.zeros_like(acc)

    w_gate = w_ref[:, 0, 0].reshape(width, units)
    w_up = w_ref[:, 0, 1].reshape(width, units)
    span = min(256, rows)
    for start in range(0, rows, span):
        at = slice(start, start + span)
        g, u = dot_nn(x_ref[at, :], w_gate), dot_nn(x_ref[at, :], w_up)
        _, gate = gate_of(gates_ref, at, span, step + first)
        hid[at, :] = (gate * (g / (1.0 + jnp.exp(-g)) * u)).astype(BF)
        pre_ref[0, at, :] = g.astype(BF)
        up_ref[0, at, :] = u.astype(BF)

    w_down = w_ref[:, 0, 2].reshape(width, units)
    part = width // n_col
    for s in range(n_col):
        cols = slice(s * part, (s + 1) * part)
        acc[:, cols] += dot_nt(hid[...], w_down[cols, :])

    @pl.when(step == pl.num_programs(0) - 1)
    def _():
        for s in range(n_col):
            total = acc[:, s * part : (s + 1) * part]
            if closing:
                total = total + first_ref[s].astype(F32)
            out_ref[s] = total.astype(BF)


def once(shape):
    return pl.BlockSpec(shape, lambda e: (0,) * len(shape), pipeline_mode=pl.Buffered(1))


def each(shape):
    return pl.BlockSpec((1, *shape), lambda e: (e,) + (0,) * len(shape))


def moe_forward(first, x, gates, weights, before):
    rows, width = x.shape
    n_row, here, _, depth, units = weights.shape
    n_col = lax.axis_size("col")
    block = pl.BlockSpec((n_row, 1, 3, depth, units), lambda e: (0, e, 0, 0, 0))
    blocks = (n_col, rows, width // n_col)
    more = [] if before is None else [before]
    hidden = jax.ShapeDtypeStruct((here, rows, units), BF)
    return pl.pallas_call(
        functools.partial(forward_kernel, first, n_col, before is not None),
        grid=(here,),
        in_specs=[once((rows, width)), once(gates.shape), block] + [once(a.shape) for a in more],
        out_specs=[once(blocks), each((rows, units)), each((rows, units))],
        out_shape=[jax.ShapeDtypeStruct(blocks, BF), hidden, hidden],
        scratch_shapes=[pltpu.VMEM((rows, width), F32)]
        + [pltpu.VMEM((rows, units), BF)],
        compiler_params=pltpu.CompilerParams(vmem_limit_bytes=VMEM_LIMIT),
        cost_estimate=pl.CostEstimate(
            flops=6 * here * rows * width * units,
            bytes_accessed=6 * here * n_row * depth * units + 8 * rows * width,
            transcendentals=here * rows * units,
        ),
        name="experts_forward",
    )(x, gates, weights, *more)


def backward_kernel(
    first, n_col, closing, xt_ref, y_ref, yt_ref, gates_ref, w_ref, pre_ref, up_ref, *rest
):
    if closing:
        probs_ref, before_ref, router_ref, first_ref, *rest = rest
    parts_ref, dx_ref, dw_ref, dg_ref, got_ref, acc, hid, d_pre, d_up, sems = rest
    step = pl.program_id(0)
    rows, width = y_ref.shape
    me = lax.axis_index("col")

    def part_copy(k):
        other = lax.rem(me + k, n_col)
        count = rows // 2
        return pltpu.make_async_remote_copy(
            src_ref=parts_ref.at[other, pl.ds(count if closing else 0, count)], dst_ref=got_ref.at[k - 1], send_sem=sems.at[0, k - 1],
            recv_sem=sems.at[1, k - 1], device_id={"col": other},
            device_id_type=pl.DeviceIdType.MESH,
        )

    @pl.when(step == 0)
    def _():
        barrier = pltpu.get_barrier_semaphore()
        for k in range(1, n_col):
            pl.semaphore_signal(
                barrier, inc=1, device_id={"col": lax.rem(me + k, n_col)},
                device_id_type=pl.DeviceIdType.MESH,
            )
        pl.semaphore_wait(barrier, n_col - 1)
        for k in range(1, n_col):
            part_copy(k).start()

    @pl.when(step == pl.num_programs(0) - 1)
    def _():
        for k in range(1, n_col):
            part_copy(k).wait()

    n_row, _, _, depth, units = w_ref.shape

    @pl.when(step == 0)
    def _():
        acc[...] = jnp.zeros_like(acc)
        dg_ref[...] = before_ref[...] if closing else jnp.zeros_like(dg_ref)

    w_gate = w_ref[:, 0, 0].reshape(width, units)
    w_up = w_ref[:, 0, 1].reshape(width, units)
    w_down = w_ref[:, 0, 2].reshape(width, units)
    span = min(256, rows)

    for start in range(0, rows, span):
        at = slice(start, start + span)
        dh = dot_nn(y_ref[at, :], w_down)
        g, u = pre_ref[0, at, :].astype(F32), up_ref[0, at, :].astype(F32)
        mine, gate = gate_of(gates_ref, at, span, step + first)
        s = 1.0 / (1.0 + jnp.exp(-g))
        silu = g * s
        both = silu * u
        hid[at, :] = (gate * both).astype(BF)
        d_gate = jnp.sum(dh * both, axis=1, keepdims=True)
        dg_ref[at, :] += jnp.where(mine, d_gate, 0.0)
        act = dh * gate
        d_pre[at, :] = (act * u * (s * (1.0 + g * (1.0 - s)))).astype(BF)
        d_up[at, :] = (act * silu).astype(BF)

    dw_ref[:, 0, 0] = dot_nn(xt_ref[...], d_pre[...]).astype(BF).reshape(n_row, depth, units)
    dw_ref[:, 0, 1] = dot_nn(xt_ref[...], d_up[...]).astype(BF).reshape(n_row, depth, units)
    dw_ref[:, 0, 2] = dot_nn(yt_ref[...], hid[...]).astype(BF).reshape(n_row, depth, units)
    part = width // n_col
    for s in range(n_col):
        cols = slice(s * part, (s + 1) * part)
        acc[:, cols] += dot_nt(d_pre[...], w_gate[cols, :]) + dot_nt(d_up[...], w_up[cols, :])

    @pl.when(step == pl.num_programs(0) - 1)
    def _():
        if closing:
            probs = probs_ref[...]
            g = jnp.where(gates_ref[...] > 0.0, dg_ref[...], 0.0)
            low = (probs * (g - jnp.sum(probs * g, axis=1, keepdims=True))).astype(BF)
        for s in range(n_col):
            cols = slice(s * part, (s + 1) * part)
            total = acc[:, cols]
            if closing:
                total = total + dot_nn(low, router_ref[:, cols]) + first_ref[s].astype(F32)
            dx_ref[s] = total.astype(BF)


def moe_backward(first, xt, y, yt, gates, weights, pre, up, parts, closing):
    rows, width = y.shape
    n_row, here, _, depth, units = weights.shape
    n_col = lax.axis_size("col")
    block = pl.BlockSpec((n_row, 1, 3, depth, units), lambda e: (0, e, 0, 0, 0))
    blocks = (n_col, rows, width // n_col)
    any_place = pl.BlockSpec(memory_space=pl.ANY)
    more = list(closing or ())
    more_specs = [once(a.shape) for a in more] + [any_place]
    more.append(parts)
    got = [jax.ShapeDtypeStruct((n_col - 1, rows // 2, width // n_col), BF)]
    sems = [pltpu.SemaphoreType.DMA((2, n_col - 1))]
    extra = {"collective_id": 5 if closing is None else 6, "has_side_effects": True}
    return pl.pallas_call(
        functools.partial(backward_kernel, first, n_col, closing is not None),
        grid=(here,),
        in_specs=[
            once((width, rows)), once((rows, width)), once((width, rows)), once(gates.shape),
            block, each((rows, units)), each((rows, units)),
        ]
        + more_specs,
        out_specs=[once(blocks), block, once(gates.shape), any_place],
        out_shape=[
            jax.ShapeDtypeStruct(blocks, BF), jax.ShapeDtypeStruct(weights.shape, BF),
            jax.ShapeDtypeStruct(gates.shape, F32),
        ]
        + got,
        scratch_shapes=[pltpu.VMEM((rows, width), F32)]
        + [pltpu.VMEM((rows, units), BF)] * 3
        + sems,
        compiler_params=pltpu.CompilerParams(vmem_limit_bytes=VMEM_LIMIT, **extra),
        cost_estimate=pl.CostEstimate(
            flops=12 * here * rows * width * units,
            bytes_accessed=12 * here * n_row * depth * units + 12 * rows * width,
            transcendentals=here * rows * units,
        ),
        name="experts_backward",
    )(xt, y, yt, gates, weights, pre, up, *more)


def pack_experts(w_gate, w_up, w_down, first, last):
    pick = lambda w: jnp.transpose(w[:, first:last], (1, 0, 2))
    return row_major(jnp.stack([pick(w_gate), pick(w_up), pick(w_down)], axis=1))


def shards(
    tokens, norm_attn, norm_query, norm_key, norm_moe, w_query, w_key, w_value, w_out, w_router,
    w_gate, w_up, w_down, routes, span_starts, cotangent,
):
    rows, part = tokens.shape
    n_col = lax.axis_size("col")
    me = lax.axis_index("col")
    width = part * n_col
    experts = w_gate.shape[1]
    half = experts // 2
    cols = w_router.shape[1]

    pad = (-(4 * part + cols)) % 128
    mats = jnp.concatenate(
        [w_query, w_key, w_value, w_out, w_router, jnp.zeros((w_router.shape[0], pad), BF)], axis=1
    )
    mats = lax.all_gather(mats, "row", axis=0, tiled=True)
    full_qkv = mats[:, : 3 * part]
    full_out = mats[:, 3 * part : 4 * part]
    first_half = lax.all_gather(pack_experts(w_gate, w_up, w_down, 0, half), "row", axis=0)
    second_half = lax.all_gather(pack_experts(w_gate, w_up, w_down, half, experts), "row", axis=0)

    attn_gain = norm_attn.reshape(1, part)
    normed_attn, inv_first = norm_line(tokens, attn_gain, width)
    qkv = dot_nn(normed_attn, full_qkv)
    query_raw, key_raw = qkv[:, :part], qkv[:, part : 2 * part]

    squares = sum_small(
        jnp.stack([jnp.sum(query_raw * query_raw, axis=1), jnp.sum(key_raw * key_raw, axis=1)])
    )
    inv_qk = lax.rsqrt(squares / width + EPSILON)
    query_inv, key_inv = inv_qk[0][:, None], inv_qk[1][:, None]
    query_gain, key_gain = norm_query.reshape(1, part), norm_key.reshape(1, part)
    cosine, sine = rope_tables(rows)
    span_of = span_ids(span_starts[0], rows)
    span_row, span_col = span_of[None, :], span_of[:, None]
    queries, keys, values, mixed = attend(
        qkv, query_inv, key_inv, query_gain, key_gain, cosine, sine, span_row, span_col
    )

    moe_gain = norm_moe.reshape(1, part)
    normed_moe, hidden_state, inv_second = attn_line(mixed, full_out, tokens, moe_gain, width)
    grad_pieces = pieces_line(cotangent + zero_of(normed_moe))

    router_t = gather_small(mats[:, 4 * part : 4 * part + cols].T).reshape(experts, width)
    router_probs = jax.nn.softmax(dot_nt(normed_moe, router_t), axis=1)
    expert_ids = jnp.arange(experts, dtype=jnp.int32)
    routed = jnp.any(routes[:, :, None] == expert_ids[None, None, :], axis=1)
    gate_table = jnp.where(routed, router_probs, 0.0)

    part_a, pre_a, up_a = moe_forward(0, normed_moe, gate_table, first_half, None)
    moe_parts, pre_b, up_b = moe_forward(half, normed_moe, gate_table, second_half, part_a)
    normed_moe_t, grad_full, grad_full_t = prepare(normed_moe, cotangent, grad_pieces, up_b)
    dx_a, dw_a, dg_a, parts_a = moe_backward(
        0, normed_moe_t, grad_full, grad_full_t, gate_table, first_half, pre_a, up_a, moe_parts,
        None,
    )
    dx_b, dw_b, dg_b, parts_b = moe_backward(
        half, normed_moe_t, grad_full, grad_full_t, gate_table, second_half, pre_b, up_b,
        moe_parts, (router_probs, dg_a, router_t, dx_a),
    )
    summed_a = lax.psum_scatter(dw_a, "row", scatter_dimension=0)
    summed_b = lax.psum_scatter(dw_b, "row", scatter_dimension=0)
    attn_grad, hidden_grad, d_moe_gain = moe_line(
        dx_b, hidden_state, inv_second, moe_gain, cotangent, width
    )
    mixed_grad = dot_nn(attn_grad, full_out).astype(BF)
    d_out_w = dot_tn(attn_grad, mixed)

    query_turned, key_turned, value_grad = attend_back(
        queries, keys, values, mixed_grad, cosine, sine, span_row, span_col, summed_a
    )
    query_scaled = query_turned * query_gain.astype(F32)
    key_scaled = key_turned * key_gain.astype(F32)
    stats = sum_small(
        jnp.stack(
            [jnp.sum(query_scaled * query_raw, axis=1), jnp.sum(key_scaled * key_raw, axis=1)]
        )
    )
    d_query_gain = jnp.sum(query_turned * query_raw * query_inv, axis=0)
    d_key_gain = jnp.sum(key_turned * key_raw * key_inv, axis=0)
    query_raw_grad = (
        query_inv * query_scaled - query_inv**3 * query_raw * stats[0][:, None] / width
    ).astype(BF)
    key_raw_grad = (
        key_inv * key_scaled - key_inv**3 * key_raw * stats[1][:, None] / width
    ).astype(BF)
    qkv_grad = jnp.concatenate([query_raw_grad, key_raw_grad, value_grad], axis=1)
    d_tokens, d_attn_gain = input_line(
        qkv_grad, mats, tokens, inv_first, attn_gain, hidden_grad, width
    )
    d_qkv_w = dot_tn(normed_attn, qkv_grad)

    gate_grad = jnp.where(routed, sum_small(dg_b.T + zero_of(attn_grad), zero_of(query_turned)).T, 0.0)
    logit_low = (
        router_probs * (gate_grad - jnp.sum(router_probs * gate_grad, axis=1, keepdims=True))
    ).astype(BF)
    d_router_w = dot_tn(normed_moe, lax.dynamic_slice_in_dim(logit_low, me * cols, cols, 1))

    spare = jnp.zeros((width, -cols % 128), BF)
    d_mats = jnp.concatenate(
        [d_qkv_w.astype(BF), d_out_w.astype(BF), d_router_w.astype(BF), spare], axis=1
    )
    summed = lax.psum_scatter(
        row_major(d_mats), "row", scatter_dimension=0, tiled=True
    ).astype(F32)
    own_part = lax.dynamic_index_in_dim(moe_parts, me, 0, keepdims=False).astype(F32)
    other_parts = jnp.concatenate([parts_a, parts_b], axis=1) + zero_of(d_tokens)
    output = (hidden_state + own_part + jnp.sum(other_parts.astype(F32), axis=0)).astype(BF)

    gains = lax.psum(jnp.stack([d_attn_gain[0], d_query_gain, d_key_gain, d_moe_gain[0]]), "row")
    expert_grads = jnp.concatenate([summed_a, summed_b], axis=0) + zero_of(d_tokens)
    unpack = lambda i: jnp.transpose(expert_grads[:, i], (1, 0, 2)).astype(F32)
    cut = lambda i: summed[:, i * part : (i + 1) * part]
    return (
        output, d_tokens, gains[0], gains[1], gains[2], gains[3],
        cut(0), cut(1), cut(2), cut(3), summed[:, 4 * part : 4 * part + cols],
        unpack(0), unpack(1), unpack(2),
    )


def solution(mesh):
    grid = P("row", "col")
    cube = P("row", None, "col")
    rows = P("row", None)
    line = P("col")
    in_specs = (
        grid, line, line, line, line, grid, grid, grid, grid, grid,
        cube, cube, cube, rows, rows, grid,
    )
    out_specs = (
        grid, grid, line, line, line, line, grid, grid, grid, grid, grid, cube, cube, cube,
    )
    return jax.shard_map(shards, mesh=mesh, in_specs=in_specs, out_specs=out_specs, check_vma=False)
```
